32 devices in a mesh: wave: 32 (over z, y, x, core), lev: 1.
Axes of the slice: x: 2, y: 2, z: 4, core: 2. Of those that a mesh axis runs over, the one named last changes fastest.
Arguments:
- grid_adjoint: bfloat16 [3, 4, 128, 1536], P(None, 'lev', 'wave'), may hold values from -6 to 6
- courant: bfloat16 [4, 128, 1536], P('lev', 'wave'), may hold values from -0.8984375 to 0.8984375
- row_points: int32 [128], P('wave'), may hold values from 20 to 1536, as said below
- wave_order: int32 [512], replicated, may hold values from 0 to 511, as said below
- legendre: bfloat16 [512, 512, 128], P('wave', 'lev'), may hold values from -0.013671875 to 0.013671875
- vert_inverse: float32 [3, 4, 4], replicated, as said below
Outputs:
- spectral_adjoint: float32 [3, 4, 512, 2, 512], P(None, None, ('wave', 'lev'))
The draws below stay inside these ranges and needn't reach their ends.
Inputs may be any that keep to these rules, and one draw needn't show every extreme that they name: Row j has row_points[j] grid points; positions at or beyond it are unused. `wave_order`: A permutation of the wavenumbers 0 to 511 in which slots 2 i and 2 i + 1 hold wavenumbers that sum to 511. `vert_inverse`: each field's matrix has diagonal entries between 0.5 and 2 plus a dense coupling of independent entries.
All inputs are finite; a program needn't handle non-finite values.
Results may differ from the reference program's by a relative error of at most 0.0047.
Values may be sent and summed in bfloat16 or wider, within the bound.
No kernel may reach another device: no remote copies, remote signals or barrier semaphores. Data moves between devices by JAX's collectives and lax.ppermute only.
A program may use at most 64 MiB of HBM per device.

```python
import math
import jax
import jax.numpy as jnp
from jax import lax

NLON = 1536
M = 512
LEV = 4
NLAT = 128


def draw_row_points(key, part):
    latitude = jnp.arange(NLAT, dtype=jnp.int32)
    distance = jnp.minimum(latitude, NLAT - 1 - latitude)
    extra = jax.random.randint(jax.random.fold_in(key, 11), (NLAT,), 0, 8, dtype=jnp.int32)
    return jnp.minimum(NLON, 20 + (2 * distance + extra) * NLON // NLAT).astype(jnp.int32)


def draw_wave_order(key, part):
    lower = jax.random.permutation(jax.random.fold_in(key, 23), M // 2).astype(jnp.int32)
    paired = jnp.stack([lower, M - 1 - lower], axis=1)
    return paired.reshape(M).astype(jnp.int32)


def draw_vert_inverse(key, part):
    first_key, second_key = jax.random.split(jax.random.fold_in(key, 37))
    diagonal = jnp.exp(jax.random.uniform(first_key, (3, LEV), jnp.float32, jnp.log(0.5), jnp.log(2.0)))
    coupling = jax.random.normal(second_key, (3, LEV, LEV), jnp.float32) * (0.5 / jnp.sqrt(LEV * 1.0))
    identity = jnp.eye(LEV, dtype=jnp.float32)
    return (coupling + identity[None] * diagonal[:, :, None]).astype(jnp.float32)


def steps_of(own_key, extent, cuts, smallest, high):
    gain, own = 1.0, jax.random.fold_in(own_key, 6)
    for axis_at, blocks in cuts:
        draws = jnp.exp(jax.random.uniform(jax.random.fold_in(own, axis_at), (blocks,), jnp.float32, smallest / len(cuts), high / len(cuts)))
        gain = gain * jnp.repeat(draws, extent[axis_at] // blocks).reshape([-1 if axis == axis_at else 1 for axis in range(len(extent))])
    return gain


def centred(key, shape, scale, most, shards=(), kind=jnp.bfloat16):
    drawn = jax.random.normal(key, shape, jnp.float32) * scale
    if len(shards) > 0:
        drawn = steps_of(key, shape, shards, -0.22, 0.18) * drawn
    return jnp.clip(drawn, min=-most, max=most).astype(kind)


def setup_inputs(seed: int = 0) -> dict:
    seeds = jax.random.split(jax.random.key(seed), 7)
    return {
        "grid_adjoint": centred(seeds[0], (3, LEV, NLAT, NLON), 1.0, 6.0, ((2, 32),)),
        "courant": jnp.clip(jax.random.uniform(seeds[1], (LEV, NLAT, NLON), jnp.float32, -0.8984375, 0.8984375) * steps_of(seeds[1], (LEV, NLAT, NLON), ((1, 32),), -0.4, 0.0), -0.8984375, 0.8984375).astype(jnp.bfloat16),
        "row_points": draw_row_points(jax.random.fold_in(seeds[6], 71), 0),
        "wave_order": draw_wave_order(jax.random.fold_in(seeds[6], 71), 0),
        "legendre": centred(seeds[4], (M, M, NLAT), (NLAT * NLON) ** -0.5, 0.013671875, ((0, 32),)),
        "vert_inverse": draw_vert_inverse(jax.random.fold_in(seeds[6], 71), 0),
    }


TWO_PI = 2.0 * math.pi


def advect(grid_rows, wind_rows, points):
    row_width = grid_rows.shape[-1]
    positions = jnp.arange(row_width, dtype=jnp.int32)
    counts = points[:, None]
    inside = positions[None, :] < counts
    at_end = positions[None, :] == counts - 1
    mass_flux = jnp.where(inside, wind_rows.astype(jnp.float32)[None] * grid_rows.astype(jnp.float32), 0.0)
    first_flux = mass_flux[..., :1]
    last_flux = jnp.sum(jnp.where(at_end, mass_flux, 0.0), axis=-1, keepdims=True)
    forward_flux = jnp.where(at_end, first_flux, jnp.roll(mass_flux, -1, axis=-1))
    backward_flux = jnp.where(positions == 0, last_flux, jnp.roll(mass_flux, 1, axis=-1))
    result = jnp.where(inside, grid_rows.astype(jnp.float32) + 0.5 * (forward_flux - backward_flux), 0.0)
    return result.astype(jnp.bfloat16)


def fourier_table(points, orders, row_width):
    positions = jnp.arange(row_width, dtype=jnp.int32)
    counts = points[:, None, None]
    phase_index = (orders[None, None, :] * positions[None, :, None]) % counts
    angles = phase_index.astype(jnp.float32) * (TWO_PI / counts.astype(jnp.float32))
    highest = (counts - 1) // 2
    factor = jnp.where(orders[None, None, :] > highest, 0.0, jnp.where(orders[None, None, :] == 0, 1.0, 2.0)).astype(jnp.float32)
    cosines = jnp.stack([jnp.cos(angles) * factor, -jnp.sin(angles) * factor], axis=-1)
    return cosines.reshape(points.shape[0], row_width, 2 * orders.shape[0]).astype(jnp.bfloat16)


def reference(grid_adjoint, courant, row_points, wave_order, legendre, vert_inverse):
    fields, levels, row_count, row_width = grid_adjoint.shape
    row_group = math.gcd(4, row_count)

    def row_block(start):
        grid_rows = lax.dynamic_slice_in_dim(grid_adjoint, start, row_group, 2)
        wind_rows = lax.dynamic_slice_in_dim(courant, start, row_group, 1)
        points = lax.dynamic_slice_in_dim(row_points, start, row_group, 0)
        advected = advect(grid_rows, wind_rows, points)
        cosines = fourier_table(points, wave_order, row_width)
        return jnp.einsum('flgk,gkc->gflc', advected.astype(jnp.float32), cosines.astype(jnp.float32))

    starts = jnp.arange(0, row_count, row_group, dtype=jnp.int32)
    fourier = lax.map(row_block, starts)
    fourier = fourier.reshape(row_count, fields, levels, -1).astype(jnp.bfloat16)
    fourier = jnp.transpose(fourier, (2, 1, 3, 0))
    wave_total = wave_order.shape[0]
    slot_group = math.gcd(16, wave_total)
    degrees = jnp.arange(wave_total, dtype=jnp.int32)

    def wave_block(start):
        fourier_part = lax.dynamic_slice_in_dim(fourier, start * 2, slot_group * 2, 2)
        fourier_part = fourier_part.reshape(levels * fields, slot_group, 2, row_count)
        legendre_rows = lax.dynamic_slice_in_dim(legendre, start, slot_group, 0)
        orders = lax.dynamic_slice_in_dim(wave_order, start, slot_group, 0)
        masked = jnp.where(degrees[None, :, None] >= orders[:, None, None], legendre_rows, jnp.zeros((), legendre_rows.dtype))
        partial_value = jnp.einsum('picj,inj->ipcn', fourier_part.astype(jnp.float32), masked.astype(jnp.float32))
        partial_value = partial_value.reshape(slot_group, levels, fields, 2, wave_total)
        return jnp.einsum('fpl,ipfcn->flicn', vert_inverse, partial_value, precision=lax.Precision.HIGHEST)

    results = lax.map(wave_block, jnp.arange(0, wave_total, slot_group, dtype=jnp.int32))
    results = jnp.transpose(results, (1, 2, 0, 3, 4, 5))
    return results.reshape(fields, levels, wave_total, 2, wave_total)
```

```python
import math

import jax
import jax.numpy as jnp
from jax import lax
from jax.experimental import pallas as pl
from jax.experimental.pallas import tpu as pltpu
from jax.sharding import PartitionSpec as P

LANES = 128
K_LOW = 32
K_TILE = 256
SIN_COEFFS = tuple(
    (-1.0) ** i * (2.0 * math.pi) ** (2 * i + 1) / math.factorial(2 * i + 1) for i in range(6)
)


def sin_quarter(v):
    s = v * v
    acc = jnp.full_like(s, SIN_COEFFS[5])
    for c in SIN_COEFFS[4::-1]:
        acc = acc * s + c
    return acc * v


def cos_sin(product, count, inverse):
    turns = jnp.floor(product * inverse + 0.5)
    u = (product - turns * count) * inverse
    cosine = sin_quarter(0.25 - jnp.abs(u))
    sine = sin_quarter(jnp.maximum(jnp.minimum(u, 0.5 - u), -0.5 - u))
    return cosine, sine


def grid_kernel(
    mix, pad, points_ref, vert_ref, grid_ref, wind_ref, order_ref, out_ref,
    x_ref, e_ref, twc_ref, tws_ref, ac_ref, as_ref,
):
    fields, levels, rows, width = grid_ref.shape
    wave_total = order_ref.shape[1]
    groups = wave_total // LANES
    pairs = fields * levels
    tiles = width // LANES

    row_id = lax.broadcasted_iota(jnp.int32, (rows, width), 0)
    positions = lax.broadcasted_iota(jnp.int32, (rows, width), 1)
    counts = jnp.zeros((rows, width), jnp.int32)
    for j in range(rows):
        counts = jnp.where(row_id == j, points_ref[j], counts)
    inside = positions < counts
    at_end = positions == counts - 1
    at_start = positions == 0
    advected = {}
    for level in range(levels):
        wind = wind_ref[level].astype(jnp.float32)
        for field in range(fields):
            g = grid_ref[field, level].astype(jnp.float32)
            flux = jnp.where(inside, wind * g, 0.0)
            first = flux[:, :1]
            last = jnp.sum(jnp.where(at_end, flux, 0.0), axis=-1, keepdims=True)
            forward = jnp.where(at_end, first, pltpu.roll(flux, width - 1, 1))
            backward = jnp.where(at_start, last, pltpu.roll(flux, 1, 1))
            result = jnp.where(inside, g + 0.5 * (forward - backward), 0.0)
            advected[field, level] = result.astype(jnp.bfloat16).astype(jnp.float32)
    for field in range(fields):
        for level in range(levels):
            if mix:
                value = vert_ref[field, 0, level] * advected[field, 0]
                for p in range(1, levels):
                    value = value + vert_ref[field, p, level] * advected[field, p]
            else:
                value = advected[field, level]
            for t in range(tiles):
                x_ref[t, pl.ds(field * levels + level, rows, stride=pad), :] = value[
                    :, t * LANES:(t + 1) * LANES
                ]
    for extra in range(pairs, pad):
        for t in range(tiles):
            x_ref[t, pl.ds(extra, rows, stride=pad), :] = jnp.zeros((rows, LANES), jnp.float32)

    shape = (rows * groups, width)
    tw_row = lax.broadcasted_iota(jnp.int32, shape, 0)
    tw_count = jnp.zeros(shape, jnp.int32)
    for j in range(rows):
        tw_count = jnp.where(tw_row // groups == j, points_ref[j], tw_count)
    tw_count = tw_count.astype(jnp.float32)
    tw_product = (
        (tw_row % groups) * LANES * lax.broadcasted_iota(jnp.int32, shape, 1)
    ).astype(jnp.float32)
    twc, tws = cos_sin(tw_product, tw_count, 1.0 / tw_count)
    twc_ref[...] = twc
    tws_ref[...] = tws

    k_high = width // K_LOW
    high = (
        K_LOW
        * lax.broadcasted_iota(jnp.int32, (k_high, LANES), 0)
        * lax.broadcasted_iota(jnp.int32, (k_high, LANES), 1)
    ).astype(jnp.float32)
    low = (
        lax.broadcasted_iota(jnp.int32, (K_LOW, LANES), 0)
        * lax.broadcasted_iota(jnp.int32, (K_LOW, LANES), 1)
    ).astype(jnp.float32)
    for j in range(rows):
        count = jnp.full((8, LANES), points_ref[j], jnp.int32).astype(jnp.float32)
        inverse = (1.0 / count)[:1]
        count = count[:1]
        ac, as_ = cos_sin(high, count, inverse)
        ac_ref[j] = ac
        as_ref[j] = as_
        bc, bs = cos_sin(low, count, inverse)
        acc = jnp.zeros(((2 * groups - 1) * pad, 2 * LANES), jnp.float32)
        for start in range(0, width, K_TILE):
            pieces = []
            for k1 in range(start // K_LOW, (start + K_TILE) // K_LOW):
                hc = ac_ref[j, pl.ds(k1, 1), :]
                hs = as_ref[j, pl.ds(k1, 1), :]
                cosine = (hc * bc - hs * bs).astype(jnp.bfloat16)
                sine = (hs * bc + hc * bs).astype(jnp.bfloat16)
                pieces.append(jnp.concatenate([cosine, sine], axis=1))
            table = jnp.concatenate(pieces, axis=0)
            x = jnp.concatenate(
                [
                    x_ref[t, pl.ds(j * pad, pad), :]
                    for t in range(start // LANES, (start + K_TILE) // LANES)
                ],
                axis=1,
            )
            left = [x.astype(jnp.bfloat16)]
            for g in range(1, groups):
                left.append(
                    (x * twc_ref[pl.ds(j * groups + g, 1), pl.ds(start, K_TILE)]).astype(jnp.bfloat16)
                )
                left.append(
                    (x * tws_ref[pl.ds(j * groups + g, 1), pl.ds(start, K_TILE)]).astype(jnp.bfloat16)
                )
            acc = acc + jnp.dot(
                jnp.concatenate(left, axis=0), table, preferred_element_type=jnp.float32
            )
        highest = (points_ref[j] - 1) // 2
        for g in range(groups):
            order = g * LANES + lax.broadcasted_iota(jnp.int32, (pad, LANES), 1)
            factor = jnp.where(order > highest, 0.0, jnp.where(order == 0, 1.0, 2.0))
            if g == 0:
                real = acc[:pad, :LANES]
                imag = acc[:pad, LANES:]
            else:
                at = (2 * g - 1) * pad
                real = acc[at:at + pad, :LANES] - acc[at + pad:at + 2 * pad, LANES:]
                imag = acc[at + pad:at + 2 * pad, :LANES] + acc[at:at + pad, LANES:]
            e_ref[g, pl.ds(j * 2 * pad, pad, stride=2), :] = real * factor
            e_ref[g, pl.ds(j * 2 * pad + 1, pad, stride=2), :] = -imag * factor

    select = (
        lax.broadcasted_iota(jnp.int32, (wave_total, wave_total), 0) == order_ref[...]
    ).astype(jnp.float32).astype(jnp.bfloat16)
    fourier = jnp.concatenate([e_ref[g].astype(jnp.bfloat16) for g in range(groups)], axis=1)
    slots = jnp.dot(fourier, select, preferred_element_type=jnp.float32)
    out_ref[...] = slots.T.astype(jnp.bfloat16)


def spectral_kernel(
    axes, sources, pad, order_ref, recv_ref, table_ref, out_ref, g_ref,
):
    step = pl.program_id(0)
    peers, fields, levels, block, _, wave_total = out_ref.shape
    lanes = recv_ref.shape[-1]
    slot_count = recv_ref.shape[1] // sources
    rows = lanes // (2 * pad)
    row_total = table_ref.shape[-1]

    @pl.when(step == 0)
    def _():
        g_ref[...] = recv_ref[...].astype(jnp.float32)

    shard = lax.axis_index(axes[0]) * lax.axis_size(axes[1]) + lax.axis_index(axes[1])
    first_slot = shard * slot_count
    spread = (
        lax.broadcasted_iota(jnp.int32, (sources, row_total), 0)
        == lax.broadcasted_iota(jnp.int32, (sources, row_total), 1) // rows
    ).astype(jnp.float32).astype(jnp.bfloat16)
    lane_row = lax.broadcasted_iota(jnp.int32, (2 * pad, row_total), 1) % rows
    degrees = lax.broadcasted_iota(jnp.int32, (2 * pad, wave_total), 1)
    for b in range(block):
        slot = step * block + b
        order = order_ref[first_slot + slot]
        for peer in range(peers):
            g = g_ref[peer, pl.ds(slot, sources, stride=slot_count), :]
            expanded = jnp.dot(
                g.T.astype(jnp.bfloat16), spread, preferred_element_type=jnp.float32
            )
            left = expanded[:2 * pad]
            for j in range(1, rows):
                left = jnp.where(lane_row == j, expanded[j * 2 * pad:(j + 1) * 2 * pad], left)
            value = lax.dot_general(
                left.astype(jnp.bfloat16), table_ref[b], (((1,), (1,)), ((), ())),
                preferred_element_type=jnp.float32,
            )
            value = jnp.where(degrees >= order, value, 0.0)
            for field in range(fields):
                for level in range(levels):
                    at = 2 * (field * levels + level)
                    out_ref[peer, field, level, b] = value[at:at + 2]


def body(grid_adjoint, courant, row_points, wave_order, legendre, vert_inverse):
    fields, levels_dev, row_count, row_width = grid_adjoint.shape
    wave_total = wave_order.shape[0]
    groups = wave_total // LANES
    sources = lax.axis_size("wave")
    peers = lax.axis_size("lev")
    pad = -(-fields * levels_dev // 16) * 16
    mix = peers == 1
    smem = pl.BlockSpec(memory_space=pltpu.SMEM)
    vmem = pl.BlockSpec(memory_space=pltpu.VMEM)
    lanes = row_count * 2 * pad
    send = pl.pallas_call(
        lambda *refs: grid_kernel(mix, pad, *refs),
        out_shape=jax.ShapeDtypeStruct((wave_total, lanes), jnp.bfloat16),
        in_specs=[smem, smem, vmem, vmem, vmem],
        out_specs=vmem,
        scratch_shapes=[
            pltpu.VMEM((row_width // LANES, row_count * pad, LANES), jnp.float32),
            pltpu.VMEM((groups, lanes, LANES), jnp.float32),
            pltpu.VMEM((row_count * groups, row_width), jnp.float32),
            pltpu.VMEM((row_count * groups, row_width), jnp.float32),
            pltpu.VMEM((row_count, row_width // K_LOW, LANES), jnp.float32),
            pltpu.VMEM((row_count, row_width // K_LOW, LANES), jnp.float32),
        ],
        name="grid_side",
    )(row_points, vert_inverse, grid_adjoint, courant, wave_order.reshape(1, wave_total))

    received = lax.all_to_all(send, "wave", split_axis=0, concat_axis=0, tiled=True)
    table = legendre
    received = received.reshape(1, sources, wave_total // sources, lanes)
    if peers > 1:
        table = lax.all_to_all(legendre, "lev", split_axis=0, concat_axis=1, tiled=True)
        received = lax.all_to_all(received, "lev", split_axis=2, concat_axis=0, tiled=True)
    slot_count, degrees, row_total = table.shape
    received = received.reshape(peers, sources * slot_count, lanes)
    block = math.gcd(4, slot_count)
    out = pl.pallas_call(
        lambda *refs: spectral_kernel(("wave", "lev"), sources, pad, *refs),
        grid=(slot_count // block,),
        out_shape=jax.ShapeDtypeStruct(
            (peers, fields, levels_dev, slot_count, 2, degrees), jnp.float32
        ),
        in_specs=[
            smem,
            vmem,
            pl.BlockSpec((block, degrees, row_total), lambda s: (s, 0, 0)),
        ],
        out_specs=pl.BlockSpec(
            (peers, fields, levels_dev, block, 2, degrees), lambda s: (0, 0, 0, s, 0, 0)
        ),
        scratch_shapes=[pltpu.VMEM((peers, sources * slot_count, lanes), jnp.float32)],
        name="spectral_side",
    )(wave_order, received, table)
    if mix:
        return out[0]
    out = jnp.transpose(out, (1, 0, 2, 3, 4, 5)).reshape(
        fields, peers * levels_dev, slot_count, 2, degrees
    )
    return jnp.einsum("fpl,fpicn->flicn", vert_inverse, out, precision=lax.Precision.HIGHEST)


def solution(mesh):
    return jax.shard_map(
        body,
        mesh=mesh,
        in_specs=(
            P(None, "lev", "wave", None),
            P("lev", "wave", None),
            P("wave"),
            P(),
            P("wave", "lev", None),
            P(),
        ),
        out_specs=P(None, None, ("wave", "lev"), None, None),
        check_vma=False,
    )
```

```python
import math

import jax
import jax.numpy as jnp
from jax import lax
from jax.experimental import pallas as pl
from jax.experimental.pallas import tpu as pltpu
from jax.sharding import PartitionSpec as P

LANES = 128
K_LOW = 32
K_TILE = 256
SIN_COEFFS = tuple(
    (-1.0) ** i * (2.0 * math.pi) ** (2 * i + 1) / math.factorial(2 * i + 1) for i in range(6)
)


def sin_quarter(v):
    s = v * v
    acc = jnp.full_like(s, SIN_COEFFS[5])
    for c in SIN_COEFFS[4::-1]:
        acc = acc * s + c
    return acc * v


def cos_sin(product, count, inverse):
    turns = jnp.floor(product * inverse + 0.5)
    u = (product - turns * count) * inverse
    cosine = sin_quarter(0.25 - jnp.abs(u))
    sine = sin_quarter(jnp.maximum(jnp.minimum(u, 0.5 - u), -0.5 - u))
    return cosine, sine


def grid_kernel(
    mix, pad, points_ref, vert_ref, grid_ref, wind_ref, order_ref, *rest
):
    if mix:
        table_hbm, out_ref, table_ref, *scratch, table_sem = rest
        fetch = pltpu.make_async_copy(table_hbm, table_ref, table_sem)
        fetch.start()
    else:
        out_ref, *scratch = rest
    x_ref, e_ref, twc_ref, tws_ref, ac_ref, as_ref = scratch
    fields, levels, rows, width = grid_ref.shape
    wave_total = order_ref.shape[1]
    groups = wave_total // LANES
    pairs = fields * levels
    tiles = width // LANES

    row_id = lax.broadcasted_iota(jnp.int32, (rows, width), 0)
    positions = lax.broadcasted_iota(jnp.int32, (rows, width), 1)
    counts = jnp.zeros((rows, width), jnp.int32)
    for j in range(rows):
        counts = jnp.where(row_id == j, points_ref[j], counts)
    inside = positions < counts
    at_end = positions == counts - 1
    at_start = positions == 0
    advected = {}
    for level in range(levels):
        wind = wind_ref[level].astype(jnp.float32)
        for field in range(fields):
            g = grid_ref[field, level].astype(jnp.float32)
            flux = jnp.where(inside, wind * g, 0.0)
            first = flux[:, :1]
            last = jnp.sum(jnp.where(at_end, flux, 0.0), axis=-1, keepdims=True)
            forward = jnp.where(at_end, first, pltpu.roll(flux, width - 1, 1))
            backward = jnp.where(at_start, last, pltpu.roll(flux, 1, 1))
            result = jnp.where(inside, g + 0.5 * (forward - backward), 0.0)
            advected[field, level] = result.astype(jnp.bfloat16).astype(jnp.float32)
    for field in range(fields):
        for level in range(levels):
            if mix:
                value = vert_ref[field, 0, level] * advected[field, 0]
                for p in range(1, levels):
                    value = value + vert_ref[field, p, level] * advected[field, p]
            else:
                value = advected[field, level]
            for t in range(tiles):
                x_ref[t, pl.ds(field * levels + level, rows, stride=pad), :] = value[
                    :, t * LANES:(t + 1) * LANES
                ]
    for extra in range(pairs, pad):
        for t in range(tiles):
            x_ref[t, pl.ds(extra, rows, stride=pad), :] = jnp.zeros((rows, LANES), jnp.float32)

    shape = (rows * groups, width)
    tw_row = lax.broadcasted_iota(jnp.int32, shape, 0)
    tw_count = jnp.zeros(shape, jnp.int32)
    for j in range(rows):
        tw_count = jnp.where(tw_row // groups == j, points_ref[j], tw_count)
    tw_count = tw_count.astype(jnp.float32)
    tw_product = (
        (tw_row % groups) * LANES * lax.broadcasted_iota(jnp.int32, shape, 1)
    ).astype(jnp.float32)
    twc, tws = cos_sin(tw_product, tw_count, 1.0 / tw_count)
    twc_ref[...] = twc
    tws_ref[...] = tws

    k_high = width // K_LOW
    high = (
        K_LOW
        * lax.broadcasted_iota(jnp.int32, (k_high, LANES), 0)
        * lax.broadcasted_iota(jnp.int32, (k_high, LANES), 1)
    ).astype(jnp.float32)
    low = (
        lax.broadcasted_iota(jnp.int32, (K_LOW, LANES), 0)
        * lax.broadcasted_iota(jnp.int32, (K_LOW, LANES), 1)
    ).astype(jnp.float32)
    for j in range(rows):
        count = jnp.full((8, LANES), points_ref[j], jnp.int32).astype(jnp.float32)
        inverse = (1.0 / count)[:1]
        count = count[:1]
        ac, as_ = cos_sin(high, count, inverse)
        ac_ref[j] = ac
        as_ref[j] = as_
        bc, bs = cos_sin(low, count, inverse)
        acc = jnp.zeros(((2 * groups - 1) * pad, 2 * LANES), jnp.float32)
        for start in range(0, width, K_TILE):
            pieces = []
            for k1 in range(start // K_LOW, (start + K_TILE) // K_LOW):
                hc = ac_ref[j, pl.ds(k1, 1), :]
                hs = as_ref[j, pl.ds(k1, 1), :]
                cosine = (hc * bc - hs * bs).astype(jnp.bfloat16)
                sine = (hs * bc + hc * bs).astype(jnp.bfloat16)
                pieces.append(jnp.concatenate([cosine, sine], axis=1))
            table = jnp.concatenate(pieces, axis=0)
            x = jnp.concatenate(
                [
                    x_ref[t, pl.ds(j * pad, pad), :]
                    for t in range(start // LANES, (start + K_TILE) // LANES)
                ],
                axis=1,
            )
            left = [x.astype(jnp.bfloat16)]
            for g in range(1, groups):
                left.append(
                    (x * twc_ref[pl.ds(j * groups + g, 1), pl.ds(start, K_TILE)]).astype(jnp.bfloat16)
                )
                left.append(
                    (x * tws_ref[pl.ds(j * groups + g, 1), pl.ds(start, K_TILE)]).astype(jnp.bfloat16)
                )
            acc = acc + jnp.dot(
                jnp.concatenate(left, axis=0), table, preferred_element_type=jnp.float32
            )
        highest = (points_ref[j] - 1) // 2
        for g in range(groups):
            order = g * LANES + lax.broadcasted_iota(jnp.int32, (pad, LANES), 1)
            factor = jnp.where(order > highest, 0.0, jnp.where(order == 0, 1.0, 2.0))
            if g == 0:
                real = acc[:pad, :LANES]
                imag = acc[:pad, LANES:]
            else:
                at = (2 * g - 1) * pad
                real = acc[at:at + pad, :LANES] - acc[at + pad:at + 2 * pad, LANES:]
                imag = acc[at + pad:at + 2 * pad, :LANES] + acc[at:at + pad, LANES:]
            e_ref[g, pl.ds(j * 2 * pad, pad, stride=2), :] = real * factor
            e_ref[g, pl.ds(j * 2 * pad + 1, pad, stride=2), :] = -imag * factor

    select = (
        lax.broadcasted_iota(jnp.int32, (wave_total, wave_total), 0) == order_ref[...]
    ).astype(jnp.float32).astype(jnp.bfloat16)
    fourier = jnp.concatenate([e_ref[g].astype(jnp.bfloat16) for g in range(groups)], axis=1)
    slots = jnp.dot(fourier, select, preferred_element_type=jnp.float32)
    out_ref[...] = slots.T.astype(jnp.bfloat16)
    if mix:
        fetch.wait()


def spectral_kernel(
    axes, sources, pad, groups, order_ref, recv_ref, table_ref, out_hbm, g_ref, left_ref, out_ref, sems,
):
    peers, fields, levels, slot_count, _, wave_total = out_ref.shape
    lanes = recv_ref.shape[-1]
    rows = lanes // (2 * pad)
    row_total = table_ref.shape[-1]
    g_ref[...] = recv_ref[...].astype(jnp.float32)

    spread = (
        lax.broadcasted_iota(jnp.int32, (sources, row_total), 0)
        == lax.broadcasted_iota(jnp.int32, (sources, row_total), 1) // rows
    ).astype(jnp.float32).astype(jnp.bfloat16)
    lane_row = lax.broadcasted_iota(jnp.int32, (2 * pad, row_total), 1) % rows
    for peer in range(peers):
        blocks = [
            g_ref[peer, pl.ds(slot, sources, stride=slot_count), :].T.astype(jnp.bfloat16)
            for slot in range(slot_count)
        ]
        expanded = jnp.dot(
            jnp.concatenate(blocks, axis=0), spread, preferred_element_type=jnp.float32
        )
        for slot in range(slot_count):
            at = slot * lanes
            left = expanded[at:at + 2 * pad]
            for j in range(1, rows):
                at = slot * lanes + j * 2 * pad
                left = jnp.where(lane_row == j, expanded[at:at + 2 * pad], left)
            left_ref[peer, slot] = left.astype(jnp.bfloat16)

    shard = lax.axis_index(axes[0]) * lax.axis_size(axes[1]) + lax.axis_index(axes[1])
    shape = (slot_count, order_ref.shape[1])
    own = lax.broadcasted_iota(jnp.int32, shape, 1) == (
        lax.broadcasted_iota(jnp.int32, shape, 0) + shard * slot_count
    )
    orders = jnp.where(own, order_ref[...].astype(jnp.float32), 0.0)
    orders = jnp.sum(orders, axis=1, keepdims=True).astype(jnp.int32)

    degrees = lax.broadcasted_iota(jnp.int32, (2 * pad, wave_total), 1)
    copies = []
    done = 0
    for slot in range(slot_count):
        order = orders[slot:slot + 1]
        for peer in range(peers):
            value = lax.dot_general(
                left_ref[peer, slot], table_ref[slot], (((1,), (1,)), ((), ())),
                preferred_element_type=jnp.float32,
            )
            value = jnp.where(degrees >= order, value, 0.0)
            for field in range(fields):
                for level in range(levels):
                    at = 2 * (field * levels + level)
                    out_ref[peer, field, level, slot] = value[at:at + 2]
        if slot + 1 in groups:
            at = (slice(None), slice(None), slice(None), pl.ds(done, slot + 1 - done))
            copies.append(
                pltpu.make_async_copy(out_ref.at[at], out_hbm.at[at], sems.at[len(copies)])
            )
            copies[-1].start()
            done = slot + 1
    for copy in copies:
        copy.wait()


def body(grid_adjoint, courant, row_points, wave_order, legendre, vert_inverse):
    fields, levels_dev, row_count, row_width = grid_adjoint.shape
    wave_total = wave_order.shape[0]
    groups = wave_total // LANES
    sources = lax.axis_size("wave")
    peers = lax.axis_size("lev")
    pad = -(-fields * levels_dev // 16) * 16
    mix = peers == 1
    smem = pl.BlockSpec(memory_space=pltpu.SMEM)
    vmem = pl.BlockSpec(memory_space=pltpu.VMEM)
    lanes = row_count * 2 * pad
    hbm = pl.BlockSpec(memory_space=pl.ANY)
    out_shape = [pltpu.VMEM((wave_total, lanes), jnp.bfloat16)]
    scratch = [
        pltpu.VMEM((row_width // LANES, row_count * pad, LANES), jnp.float32),
        pltpu.VMEM((groups, lanes, LANES), jnp.float32),
        pltpu.VMEM((row_count * groups, row_width), jnp.float32),
        pltpu.VMEM((row_count * groups, row_width), jnp.float32),
        pltpu.VMEM((row_count, row_width // K_LOW, LANES), jnp.float32),
        pltpu.VMEM((row_count, row_width // K_LOW, LANES), jnp.float32),
    ]
    operands = [row_points, vert_inverse, grid_adjoint, courant, wave_order.reshape(1, wave_total)]
    specs = [smem, smem, vmem, vmem, vmem]
    if mix:
        operands.append(legendre)
        specs.append(hbm)
        out_shape.append(pltpu.VMEM(legendre.shape, legendre.dtype))
        scratch.append(pltpu.SemaphoreType.DMA(()))
    send, *table = pl.pallas_call(
        lambda *refs: grid_kernel(mix, pad, *refs),
        out_shape=out_shape,
        in_specs=specs,
        out_specs=[vmem] * len(out_shape),
        scratch_shapes=scratch,
        name="grid_side",
    )(*operands)

    received = lax.all_to_all(send, "wave", split_axis=0, concat_axis=0, tiled=True)
    received = received.reshape(1, sources, wave_total // sources, lanes)
    if peers > 1:
        table = [lax.all_to_all(legendre, "lev", split_axis=0, concat_axis=1, tiled=True)]
        received = lax.all_to_all(received, "lev", split_axis=2, concat_axis=0, tiled=True)
    slot_count, degrees, row_total = table[0].shape
    received = received.reshape(peers, sources * slot_count, lanes)
    block = math.gcd(4, slot_count)
    ends = tuple(range(block, slot_count + 1, block))
    shape = (peers, fields, levels_dev, slot_count, 2, degrees)
    out = pl.pallas_call(
        lambda *refs: spectral_kernel(("wave", "lev"), sources, pad, ends, *refs),
        out_shape=jax.ShapeDtypeStruct(shape, jnp.float32),
        in_specs=[vmem, vmem, vmem],
        out_specs=hbm,
        scratch_shapes=[
            pltpu.VMEM((peers, sources * slot_count, lanes), jnp.float32),
            pltpu.VMEM((peers, slot_count, 2 * pad, row_total), jnp.bfloat16),
            pltpu.VMEM(shape, jnp.float32),
            pltpu.SemaphoreType.DMA((len(ends),)),
        ],
        compiler_params=pltpu.CompilerParams(vmem_limit_bytes=16 << 20),
        name="spectral_side",
    )(
        wave_order.reshape(1, wave_total),
        pltpu.with_memory_space_constraint(received, pltpu.VMEM),
        pltpu.with_memory_space_constraint(table[0], pltpu.VMEM),
    )
    if mix:
        return out[0]
    out = jnp.transpose(out, (1, 0, 2, 3, 4, 5)).reshape(
        fields, peers * levels_dev, slot_count, 2, degrees
    )
    return jnp.einsum("fpl,fpicn->flicn", vert_inverse, out, precision=lax.Precision.HIGHEST)


def solution(mesh):
    return jax.shard_map(
        body,
        mesh=mesh,
        in_specs=(
            P(None, "lev", "wave", None),
            P("lev", "wave", None),
            P("wave"),
            P(),
            P("wave", "lev", None),
            P(),
        ),
        out_specs=P(None, None, ("wave", "lev"), None, None),
        check_vma=False,
    )
```

```python
import math

import jax
import jax.numpy as jnp
from jax import lax
from jax.experimental import pallas as pl
from jax.experimental.pallas import tpu as pltpu
from jax.sharding import PartitionSpec as P

LANES = 128
HALF = 16
SIN_COEFFS = tuple(
    (-1.0) ** i * (2.0 * math.pi) ** (2 * i + 1) / math.factorial(2 * i + 1) for i in range(6)
)


def sin_quarter(v):
    s = v * v
    acc = SIN_COEFFS[5] * s + SIN_COEFFS[4]
    for c in SIN_COEFFS[3::-1]:
        acc = acc * s + c
    return acc * v


def cos_sin(product, count, inverse):
    turns = jnp.floor(product * inverse + 0.5)
    u = (product - turns * count) * inverse
    cosine = sin_quarter(0.25 - jnp.abs(u))
    sine = sin_quarter(jnp.maximum(jnp.minimum(u, 0.5 - u), -0.5 - u))
    return cosine, sine


def iota(shape, axis):
    return lax.broadcasted_iota(jnp.int32, shape, axis)


def within_tile(lane):
    inner = lane % (2 * HALF)
    return lane - inner + jnp.where(inner < HALF, HALF + inner, 2 * HALF - 1 - inner)


def grid_kernel(
    mix, pad, points_hbm, vert_hbm, grid_hbm, wind_hbm, order_hbm, *rest
):
    if mix:
        table_hbm, out_ref, table_ref, *scratch, table_sem = rest
        fetch = pltpu.make_async_copy(table_hbm, table_ref, table_sem)
    else:
        out_ref, *scratch = rest
    (
        grid_buf, wind_buf, g_ref, f_ref, x_ref, t_ref, e_ref,
        twc_ref, tws_ref, ac_ref, as_ref, turn_ref, mix_ref,
        points_ref, vert_ref, order_ref, points_sem, vert_sem, order_sem, grid_sem, wind_sem,
    ) = scratch
    points_copy = pltpu.make_async_copy(points_hbm, points_ref, points_sem)
    points_copy.start()
    vert_copy = pltpu.make_async_copy(vert_hbm, vert_ref, vert_sem)
    order_copy = pltpu.make_async_copy(order_hbm, order_ref, order_sem)
    grid_copy = pltpu.make_async_copy(grid_hbm, grid_buf, grid_sem)
    wind_copy = pltpu.make_async_copy(wind_hbm, wind_buf, wind_sem)
    grid_copy.start()
    wind_copy.start()
    vert_copy.start()
    order_copy.start()
    if mix:
        fetch.start()
    fields, levels, rows, width = grid_buf.shape
    wave_total = order_ref.shape[1]
    groups = wave_total // LANES
    pairs = fields * levels
    tiles = width // LANES
    half_tiles = -(-width // (2 * LANES))
    half_width = half_tiles * LANES

    points_copy.wait()

    shape = (rows * groups, half_width)
    row_id = iota(shape, 0)
    count = jnp.zeros(shape, jnp.int32)
    for j in range(rows):
        count = jnp.where(row_id // groups == j, 2 * points_ref[j], count)
    count = count.astype(jnp.float32)
    lane = iota(shape, 1)
    product = ((row_id % groups) * LANES * (2 * within_tile(lane) + 1)).astype(jnp.float32)
    twc, tws = cos_sin(product, count, 1.0 / count)
    twc_ref[...] = twc
    tws_ref[...] = tws

    shape = (max(rows, 8), wave_total)
    row_id = iota(shape, 0)
    count = jnp.full(shape, 2 * points_ref[0], jnp.int32)
    for j in range(1, rows):
        count = jnp.where(row_id == j, 2 * points_ref[j], count)
    wave = iota(shape, 1)
    weight = jnp.where(2 * wave > count // 2 - 1, 0.0, jnp.where(wave == 0, 1.0, 2.0))
    count = count.astype(jnp.float32)
    cosine, sine = cos_sin(wave.astype(jnp.float32), count, 1.0 / count)
    turn_ref[0] = cosine * weight
    turn_ref[1] = sine * weight

    blocks = half_width // (2 * HALF)
    high = (iota((blocks, LANES), 1) * (4 * HALF * iota((blocks, LANES), 0) + 2 * HALF)).astype(
        jnp.float32
    )
    low = (iota((HALF, LANES), 1) * (2 * iota((HALF, LANES), 0) + 1)).astype(jnp.float32)
    for j in range(rows):
        count = jnp.full((8, LANES), 2 * points_ref[j], jnp.int32).astype(jnp.float32)
        inverse = (1.0 / count)[:1]
        count = count[:1]
        ac, as_ = cos_sin(high, count, inverse)
        ac_ref[j] = ac
        as_ref[j] = as_
        bc, bs = cos_sin(low, count, inverse)
        for block in range(blocks):
            hc = ac_ref[j, pl.ds(block, 1), :]
            hs = as_ref[j, pl.ds(block, 1), :]
            cc, ss, sc, cs = hc * bc, hs * bs, hs * bc, hc * bs
            at = 2 * HALF * block
            t_ref[j, pl.ds(at, HALF), :] = (cc - ss).astype(jnp.bfloat16)
            t_ref[j, pl.ds(at + HALF, HALF), :] = (cc + ss).astype(jnp.bfloat16)
            at += half_width
            t_ref[j, pl.ds(at, HALF), :] = (sc + cs).astype(jnp.bfloat16)
            t_ref[j, pl.ds(at + HALF, HALF), :] = (sc - cs).astype(jnp.bfloat16)

    vert_copy.wait()
    if mix:
        mix_ref[...] = jnp.zeros_like(mix_ref)
        lane = iota((1, LANES), 1)
        for field in range(fields):
            for level in range(levels):
                row = jnp.zeros((1, LANES), jnp.float32)
                for p in range(levels):
                    hit = (lane % pad == field * levels + p) & (lane < 3 * pad)
                    row = jnp.where(hit, vert_ref[field, p, level], row)
                mix_ref[pl.ds(field * levels + level, 1), :] = row
        full = mix_ref[...]
        first = full.astype(jnp.bfloat16).astype(jnp.float32)
        second = (full - first).astype(jnp.bfloat16).astype(jnp.float32)
        third = full - first - second
        lane = iota((pad, LANES), 1)
        matrix = jnp.where(lane < pad, first, jnp.where(lane < 2 * pad, second, third))
        matrix = matrix[:, :3 * pad].astype(jnp.bfloat16)

    order_copy.wait()
    wind_copy.wait()
    grid_copy.wait()
    half_pad = pad // 2
    shape = (rows * pad, pairs * rows)
    pick = (iota(shape, 0) % pad * rows + iota(shape, 0) // pad == iota(shape, 1)) & (
        iota(shape, 0) % pad < pairs
    )
    grid_rows = jnp.dot(
        pick.astype(jnp.float32).astype(jnp.bfloat16),
        grid_buf[...].reshape(pairs * rows, width),
        preferred_element_type=jnp.float32,
    )
    shape = (rows * half_pad, levels * rows)
    pick = iota(shape, 0) % levels * rows + iota(shape, 0) // half_pad == iota(shape, 1)
    wind_rows = jnp.dot(
        jnp.where(pick, 0.5, 0.0).astype(jnp.bfloat16),
        wind_buf[...].reshape(levels * rows, width),
        preferred_element_type=jnp.float32,
    )
    for j in range(rows):
        for t in range(tiles):
            at = slice(t * LANES, (t + 1) * LANES)
            g = grid_rows[j * pad:(j + 1) * pad, at]
            w = wind_rows[j * half_pad:(j + 1) * half_pad, at]
            g_ref[j, t] = g
            f_ref[j, t + 1] = g * jnp.concatenate([w, w], axis=0)

    lane = iota((pad, LANES), 1)
    point = within_tile(lane)
    for j in range(rows):
        length = points_ref[j]
        next_tile = length // LANES
        next_lane = length % LANES
        f_ref[j, 0] = pltpu.roll(
            f_ref[j, (length - 1) // LANES + 1], LANES - 1 - (length - 1) % LANES, 1
        )
        f_ref[j, tiles + 1] = jnp.zeros((pad, LANES), jnp.float32)
        f_ref[j, next_tile + 1] = jnp.where(
            lane == next_lane, pltpu.roll(f_ref[j, 1], next_lane, 1), f_ref[j, next_tile + 1]
        )
    advected = []
    for j in range(rows):
        flux = [f_ref[j, t] for t in range(tiles + 2)]
        ahead = [pltpu.roll(f, LANES - 1, 1) for f in flux[1:]]
        behind = [pltpu.roll(f, 1, 1) for f in flux[:-1]]
        parts = []
        for t in range(tiles):
            forward = jnp.where(lane == LANES - 1, ahead[t + 1], ahead[t])
            backward = jnp.where(lane == 0, behind[t], behind[t + 1])
            parts.append((g_ref[j, t] + (forward - backward)).astype(jnp.bfloat16))
        advected.append(jnp.concatenate(parts, axis=1))
    for j in range(rows):
        if mix:
            mixed = jnp.dot(
                matrix, jnp.concatenate([advected[j]] * 3, axis=0),
                preferred_element_type=jnp.float32,
            )
        else:
            mixed = advected[j].astype(jnp.float32)
        for t in range(tiles):
            x_ref[j, half_tiles + t] = mixed[:, t * LANES:(t + 1) * LANES]

    products = []
    for j in range(rows):
        length = points_ref[j]
        last_tile = (length - 1) // LANES
        last_lane = (length - 1) % LANES
        mirror = (last_lane - point) & (LANES - 1)
        mirrored = [
            jnp.take_along_axis(x_ref[j, half_tiles + last_tile - t], mirror, axis=1)
            for t in range(half_tiles + 1)
        ]
        even = []
        odd = []
        for t in range(half_tiles):
            value = jnp.take_along_axis(x_ref[j, half_tiles + t], point, axis=1)
            other = jnp.where(point <= last_lane, mirrored[t], mirrored[t + 1])
            paired = 2 * (point + t * LANES) < length - 1
            kept = 2 * (point + t * LANES) <= length - 1
            other = jnp.where(paired, other, 0.0)
            even.append(jnp.where(kept, value, 0.0) + other)
            odd.append(jnp.where(paired, value, 0.0) - other)
        even = jnp.concatenate(even, axis=1)
        odd = jnp.concatenate(odd, axis=1)

        real = [jnp.concatenate([even.astype(jnp.bfloat16), jnp.zeros(even.shape, jnp.bfloat16)], 1)]
        imag = [jnp.concatenate([jnp.zeros(odd.shape, jnp.bfloat16), odd.astype(jnp.bfloat16)], 1)]
        for g in range(1, groups):
            c = twc_ref[pl.ds(j * groups + g, 1), :]
            s = tws_ref[pl.ds(j * groups + g, 1), :]
            real.append(
                jnp.concatenate(
                    [(even * c).astype(jnp.bfloat16), (even * -s).astype(jnp.bfloat16)], axis=1
                )
            )
            imag.append(
                jnp.concatenate(
                    [(odd * s).astype(jnp.bfloat16), (odd * c).astype(jnp.bfloat16)], axis=1
                )
            )
        left = jnp.concatenate(real + imag, axis=0)

        products.append(jnp.dot(left, t_ref[j], preferred_element_type=jnp.float32))
    for j in range(rows):
        product = products[j]
        for g in range(groups):
            yr = product[g * pad:(g + 1) * pad]
            yi = product[(groups + g) * pad:(groups + g + 1) * pad]
            c = turn_ref[0, pl.ds(j, 1), pl.ds(g * LANES, LANES)]
            s = turn_ref[1, pl.ds(j, 1), pl.ds(g * LANES, LANES)]
            e_ref[g, pl.ds(j * 2 * pad, pad, stride=2), :] = c * yr + s * yi
            e_ref[g, pl.ds(j * 2 * pad + 1, pad, stride=2), :] = s * yr - c * yi

    select = (
        iota((wave_total, wave_total), 0) == order_ref[...]
    ).astype(jnp.float32).astype(jnp.bfloat16)
    fourier = jnp.concatenate([e_ref[g].astype(jnp.bfloat16) for g in range(groups)], axis=1)
    slots = jnp.dot(fourier, select, preferred_element_type=jnp.float32)
    out_ref[...] = slots.T.astype(jnp.bfloat16)
    if mix:
        fetch.wait()


def spectral_kernel(
    axes, sources, pad, groups, order_ref, recv_ref, table_ref, out_hbm, g_ref, left_ref, out_ref, sems,
):
    peers, fields, levels, slot_count, _, wave_total = out_ref.shape
    lanes = recv_ref.shape[-1]
    rows = lanes // (2 * pad)
    row_total = table_ref.shape[-1]
    g_ref[...] = recv_ref[...].astype(jnp.float32)

    spread = (
        lax.broadcasted_iota(jnp.int32, (sources, row_total), 0)
        == lax.broadcasted_iota(jnp.int32, (sources, row_total), 1) // rows
    ).astype(jnp.float32).astype(jnp.bfloat16)
    lane_row = lax.broadcasted_iota(jnp.int32, (2 * pad, row_total), 1) % rows
    for peer in range(peers):
        blocks = [
            g_ref[peer, pl.ds(slot, sources, stride=slot_count), :].T.astype(jnp.bfloat16)
            for slot in range(slot_count)
        ]
        expanded = jnp.dot(
            jnp.concatenate(blocks, axis=0), spread, preferred_element_type=jnp.float32
        )
        for slot in range(slot_count):
            at = slot * lanes
            left = expanded[at:at + 2 * pad]
            for j in range(1, rows):
                at = slot * lanes + j * 2 * pad
                left = jnp.where(lane_row == j, expanded[at:at + 2 * pad], left)
            left_ref[peer, slot] = left.astype(jnp.bfloat16)

    shard = lax.axis_index(axes[0]) * lax.axis_size(axes[1]) + lax.axis_index(axes[1])
    shape = (slot_count, order_ref.shape[1])
    own = lax.broadcasted_iota(jnp.int32, shape, 1) == (
        lax.broadcasted_iota(jnp.int32, shape, 0) + shard * slot_count
    )
    orders = jnp.where(own, order_ref[...].astype(jnp.float32), 0.0)
    orders = jnp.sum(orders, axis=1, keepdims=True).astype(jnp.int32)

    degrees = lax.broadcasted_iota(jnp.int32, (2 * pad, wave_total), 1)
    copies = []
    done = 0
    for slot in range(slot_count):
        order = orders[slot:slot + 1]
        for peer in range(peers):
            value = lax.dot_general(
                left_ref[peer, slot], table_ref[slot], (((1,), (1,)), ((), ())),
                preferred_element_type=jnp.float32,
            )
            value = jnp.where(degrees >= order, value, 0.0)
            for field in range(fields):
                for level in range(levels):
                    at = 2 * (field * levels + level)
                    out_ref[peer, field, level, slot] = value[at:at + 2]
        if slot + 1 in groups:
            at = (slice(None), slice(None), slice(None), pl.ds(done, slot + 1 - done))
            copies.append(
                pltpu.make_async_copy(out_ref.at[at], out_hbm.at[at], sems.at[len(copies)])
            )
            copies[-1].start()
            done = slot + 1
    for copy in copies:
        copy.wait()


def body(grid_adjoint, courant, row_points, wave_order, legendre, vert_inverse):
    fields, levels_dev, row_count, row_width = grid_adjoint.shape
    wave_total = wave_order.shape[0]
    groups = wave_total // LANES
    sources = lax.axis_size("wave")
    peers = lax.axis_size("lev")
    pad = -(-fields * levels_dev // 16) * 16
    mix = peers == 1
    smem = pl.BlockSpec(memory_space=pltpu.SMEM)
    vmem = pl.BlockSpec(memory_space=pltpu.VMEM)
    lanes = row_count * 2 * pad
    hbm = pl.BlockSpec(memory_space=pl.ANY)
    out_shape = [pltpu.VMEM((wave_total, lanes), jnp.bfloat16)]
    tiles = row_width // LANES
    half_tiles = -(-row_width // (2 * LANES))
    half_width = half_tiles * LANES
    blocks = half_width // (2 * HALF)
    scratch = [
        pltpu.VMEM(grid_adjoint.shape, grid_adjoint.dtype),
        pltpu.VMEM(courant.shape, courant.dtype),
        pltpu.VMEM((row_count, tiles, pad, LANES), jnp.float32),
        pltpu.VMEM((row_count, tiles + 2, pad, LANES), jnp.float32),
        pltpu.VMEM((row_count, half_tiles + tiles, pad, LANES), jnp.float32),
        pltpu.VMEM((row_count, 2 * half_width, LANES), jnp.bfloat16),
        pltpu.VMEM((groups, lanes, LANES), jnp.float32),
        pltpu.VMEM((row_count * groups, half_width), jnp.float32),
        pltpu.VMEM((row_count * groups, half_width), jnp.float32),
        pltpu.VMEM((row_count, blocks, LANES), jnp.float32),
        pltpu.VMEM((row_count, blocks, LANES), jnp.float32),
        pltpu.VMEM((2, max(row_count, 8), wave_total), jnp.float32),
        pltpu.VMEM((pad, LANES), jnp.float32),
        pltpu.SMEM(row_points.shape, row_points.dtype),
        pltpu.SMEM(vert_inverse.shape, vert_inverse.dtype),
        pltpu.VMEM((1, wave_total), jnp.int32),
        *[pltpu.SemaphoreType.DMA(())] * 5,
    ]
    operands = [row_points, vert_inverse, grid_adjoint, courant, wave_order.reshape(1, wave_total)]
    specs = [hbm] * 5
    if mix:
        operands.append(legendre)
        specs.append(hbm)
        out_shape.append(pltpu.VMEM(legendre.shape, legendre.dtype))
        scratch.append(pltpu.SemaphoreType.DMA(()))
    send, *table = pl.pallas_call(
        lambda *refs: grid_kernel(mix, pad, *refs),
        out_shape=out_shape,
        in_specs=specs,
        out_specs=[vmem] * len(out_shape),
        scratch_shapes=scratch,
        name="grid_side",
    )(*operands)

    received = lax.all_to_all(send, "wave", split_axis=0, concat_axis=0, tiled=True)
    received = received.reshape(1, sources, wave_total // sources, lanes)
    if peers > 1:
        table = [lax.all_to_all(legendre, "lev", split_axis=0, concat_axis=1, tiled=True)]
        received = lax.all_to_all(received, "lev", split_axis=2, concat_axis=0, tiled=True)
    slot_count, degrees, row_total = table[0].shape
    received = received.reshape(peers, sources * slot_count, lanes)
    block = math.gcd(4, slot_count)
    ends = tuple(range(block, slot_count + 1, block))
    shape = (peers, fields, levels_dev, slot_count, 2, degrees)
    out = pl.pallas_call(
        lambda *refs: spectral_kernel(("wave", "lev"), sources, pad, ends, *refs),
        out_shape=jax.ShapeDtypeStruct(shape, jnp.float32),
        in_specs=[vmem, vmem, vmem],
        out_specs=hbm,
        scratch_shapes=[
            pltpu.VMEM((peers, sources * slot_count, lanes), jnp.float32),
            pltpu.VMEM((peers, slot_count, 2 * pad, row_total), jnp.bfloat16),
            pltpu.VMEM(shape, jnp.float32),
            pltpu.SemaphoreType.DMA((len(ends),)),
        ],
        compiler_params=pltpu.CompilerParams(vmem_limit_bytes=16 << 20),
        name="spectral_side",
    )(
        wave_order.reshape(1, wave_total),
        pltpu.with_memory_space_constraint(received, pltpu.VMEM),
        pltpu.with_memory_space_constraint(table[0], pltpu.VMEM),
    )
    if mix:
        return out[0]
    out = jnp.transpose(out, (1, 0, 2, 3, 4, 5)).reshape(
        fields, peers * levels_dev, slot_count, 2, degrees
    )
    return jnp.einsum("fpl,fpicn->flicn", vert_inverse, out, precision=lax.Precision.HIGHEST)


def solution(mesh):
    return jax.shard_map(
        body,
        mesh=mesh,
        in_specs=(
            P(None, "lev", "wave", None),
            P("lev", "wave", None),
            P("wave"),
            P(),
            P("wave", "lev", None),
            P(),
        ),
        out_specs=P(None, None, ("wave", "lev"), None, None),
        check_vma=False,
    )
```

```python
import math

import jax
import jax.numpy as jnp
from jax import lax
from jax.experimental import pallas as pl
from jax.experimental.pallas import tpu as pltpu
from jax.sharding import PartitionSpec as P

LANES = 128
HALF = 16
SIN_COEFFS = tuple(
    (-1.0) ** i * (2.0 * math.pi) ** (2 * i + 1) / math.factorial(2 * i + 1) for i in range(6)
)


def sin_quarter(v):
    s = v * v
    acc = SIN_COEFFS[5] * s + SIN_COEFFS[4]
    for c in SIN_COEFFS[3::-1]:
        acc = acc * s + c
    return acc * v


def cos_sin(product, count, inverse):
    turns = jnp.floor(product * inverse + 0.5)
    u = (product - turns * count) * inverse
    cosine = sin_quarter(0.25 - jnp.abs(u))
    sine = sin_quarter(jnp.maximum(jnp.minimum(u, 0.5 - u), -0.5 - u))
    return cosine, sine


def iota(shape, axis):
    return lax.broadcasted_iota(jnp.int32, shape, axis)


def within_tile(lane):
    inner = lane % (2 * HALF)
    return lane - inner + jnp.where(inner < HALF, HALF + inner, 2 * HALF - 1 - inner)


def grid_kernel(
    mix, pad, points_hbm, vert_hbm, grid_hbm, wind_hbm, order_hbm, *rest
):
    if mix:
        table_hbm, out_ref, table_ref, *scratch, table_sem = rest
        fetch = pltpu.make_async_copy(table_hbm, table_ref, table_sem)
    else:
        out_ref, *scratch = rest
    (
        grid_buf, wind_buf, g_ref, f_ref, x_ref, t_ref, e_ref,
        twc_ref, tws_ref, ac_ref, as_ref, turn_ref, mix_ref,
        points_ref, vert_ref, order_ref, points_sem, vert_sem, order_sem, grid_sem, wind_sem,
    ) = scratch
    points_copy = pltpu.make_async_copy(points_hbm, points_ref, points_sem)
    points_copy.start()
    vert_copy = pltpu.make_async_copy(vert_hbm, vert_ref, vert_sem)
    order_copy = pltpu.make_async_copy(order_hbm, order_ref, order_sem)
    grid_copy = pltpu.make_async_copy(grid_hbm, grid_buf, grid_sem)
    wind_copy = pltpu.make_async_copy(wind_hbm, wind_buf, wind_sem)
    grid_copy.start()
    wind_copy.start()
    vert_copy.start()
    order_copy.start()
    if mix:
        fetch.start()
    fields, levels, rows, width = grid_buf.shape
    wave_total = order_ref.shape[1]
    groups = wave_total // LANES
    pairs = fields * levels
    tiles = width // LANES
    half_tiles = -(-width // (2 * LANES))
    half_width = half_tiles * LANES

    points_copy.wait()

    shape = (rows * groups, half_width)
    row_id = iota(shape, 0)
    count = jnp.zeros(shape, jnp.int32)
    for j in range(rows):
        count = jnp.where(row_id // groups == j, 2 * points_ref[j], count)
    count = count.astype(jnp.float32)
    lane = iota(shape, 1)
    product = ((row_id % groups) * LANES * (2 * within_tile(lane) + 1)).astype(jnp.float32)
    twc, tws = cos_sin(product, count, 1.0 / count)
    twc_ref[...] = twc
    tws_ref[...] = tws

    shape = (max(rows, 8), wave_total)
    row_id = iota(shape, 0)
    count = jnp.full(shape, 2 * points_ref[0], jnp.int32)
    for j in range(1, rows):
        count = jnp.where(row_id == j, 2 * points_ref[j], count)
    wave = iota(shape, 1)
    weight = jnp.where(2 * wave > count // 2 - 1, 0.0, jnp.where(wave == 0, 1.0, 2.0))
    count = count.astype(jnp.float32)
    cosine, sine = cos_sin(wave.astype(jnp.float32), count, 1.0 / count)
    turn_ref[0] = cosine * weight
    turn_ref[1] = sine * weight

    blocks = half_width // (2 * HALF)
    high = (iota((blocks, LANES), 1) * (4 * HALF * iota((blocks, LANES), 0) + 2 * HALF)).astype(
        jnp.float32
    )
    low = (iota((HALF, LANES), 1) * (2 * iota((HALF, LANES), 0) + 1)).astype(jnp.float32)
    for j in range(rows):
        count = jnp.full((8, LANES), 2 * points_ref[j], jnp.int32).astype(jnp.float32)
        inverse = (1.0 / count)[:1]
        count = count[:1]
        ac, as_ = cos_sin(high, count, inverse)
        ac_ref[j] = ac
        as_ref[j] = as_
        bc, bs = cos_sin(low, count, inverse)
        for block in range(blocks):
            hc = ac_ref[j, pl.ds(block, 1), :]
            hs = as_ref[j, pl.ds(block, 1), :]
            cc, ss, sc, cs = hc * bc, hs * bs, hs * bc, hc * bs
            at = 2 * HALF * block
            t_ref[j, pl.ds(at, HALF), :] = (cc - ss).astype(jnp.bfloat16)
            t_ref[j, pl.ds(at + HALF, HALF), :] = (cc + ss).astype(jnp.bfloat16)
            at += half_width
            t_ref[j, pl.ds(at, HALF), :] = (sc + cs).astype(jnp.bfloat16)
            t_ref[j, pl.ds(at + HALF, HALF), :] = (sc - cs).astype(jnp.bfloat16)

    vert_copy.wait()
    if mix:
        mix_ref[...] = jnp.zeros_like(mix_ref)
        lane = iota((1, LANES), 1)
        for field in range(fields):
            for level in range(levels):
                row = jnp.zeros((1, LANES), jnp.float32)
                for p in range(levels):
                    hit = (lane % pad == field * levels + p) & (lane < 3 * pad)
                    row = jnp.where(hit, vert_ref[field, p, level], row)
                mix_ref[pl.ds(field * levels + level, 1), :] = row
        full = mix_ref[...]
        first = full.astype(jnp.bfloat16).astype(jnp.float32)
        second = (full - first).astype(jnp.bfloat16).astype(jnp.float32)
        third = full - first - second
        lane = iota((pad, LANES), 1)
        matrix = jnp.where(lane < pad, first, jnp.where(lane < 2 * pad, second, third))
        matrix = matrix[:, :3 * pad].astype(jnp.bfloat16)

    order_copy.wait()
    wind_copy.wait()
    grid_copy.wait()
    half_pad = pad // 2
    shape = (rows * pad, pairs * rows)
    pick = (iota(shape, 0) % pad * rows + iota(shape, 0) // pad == iota(shape, 1)) & (
        iota(shape, 0) % pad < pairs
    )
    grid_rows = jnp.dot(
        pick.astype(jnp.float32).astype(jnp.bfloat16),
        grid_buf[...].reshape(pairs * rows, width),
        preferred_element_type=jnp.float32,
    )
    shape = (rows * half_pad, levels * rows)
    pick = iota(shape, 0) % levels * rows + iota(shape, 0) // half_pad == iota(shape, 1)
    wind_rows = jnp.dot(
        jnp.where(pick, 0.5, 0.0).astype(jnp.bfloat16),
        wind_buf[...].reshape(levels * rows, width),
        preferred_element_type=jnp.float32,
    )
    for j in range(rows):
        for t in range(tiles):
            at = slice(t * LANES, (t + 1) * LANES)
            g = grid_rows[j * pad:(j + 1) * pad, at]
            w = wind_rows[j * half_pad:(j + 1) * half_pad, at]
            g_ref[j, t] = g
            f_ref[j, t + 1] = g * jnp.concatenate([w, w], axis=0)

    lane = iota((pad, LANES), 1)
    point = within_tile(lane)
    for j in range(rows):
        length = points_ref[j]
        next_tile = length // LANES
        next_lane = length % LANES
        f_ref[j, 0] = pltpu.roll(
            f_ref[j, (length - 1) // LANES + 1], LANES - 1 - (length - 1) % LANES, 1
        )
        f_ref[j, tiles + 1] = jnp.zeros((pad, LANES), jnp.float32)
        f_ref[j, next_tile + 1] = jnp.where(
            lane == next_lane, pltpu.roll(f_ref[j, 1], next_lane, 1), f_ref[j, next_tile + 1]
        )
    advected = []
    for j in range(rows):
        flux = [f_ref[j, t] for t in range(tiles + 2)]
        ahead = [pltpu.roll(f, LANES - 1, 1) for f in flux[1:]]
        behind = [pltpu.roll(f, 1, 1) for f in flux[:-1]]
        parts = []
        for t in range(tiles):
            forward = jnp.where(lane == LANES - 1, ahead[t + 1], ahead[t])
            backward = jnp.where(lane == 0, behind[t], behind[t + 1])
            parts.append((g_ref[j, t] + (forward - backward)).astype(jnp.bfloat16))
        advected.append(jnp.concatenate(parts, axis=1))
    for j in range(rows):
        if mix:
            mixed = jnp.dot(
                matrix, jnp.concatenate([advected[j]] * 3, axis=0),
                preferred_element_type=jnp.float32,
            )
        else:
            mixed = advected[j].astype(jnp.float32)
        for t in range(tiles):
            x_ref[j, half_tiles + t] = mixed[:, t * LANES:(t + 1) * LANES]

    products = []
    for j in range(rows):
        length = points_ref[j]
        last_tile = (length - 1) // LANES
        last_lane = (length - 1) % LANES
        mirror = (last_lane - point) & (LANES - 1)
        mirrored = [
            jnp.take_along_axis(x_ref[j, half_tiles + last_tile - t], mirror, axis=1)
            for t in range(half_tiles + 1)
        ]
        even = []
        odd = []
        for t in range(half_tiles):
            value = jnp.take_along_axis(x_ref[j, half_tiles + t], point, axis=1)
            other = jnp.where(point <= last_lane, mirrored[t], mirrored[t + 1])
            paired = 2 * (point + t * LANES) < length - 1
            kept = 2 * (point + t * LANES) <= length - 1
            other = jnp.where(paired, other, 0.0)
            even.append(jnp.where(kept, value, 0.0) + other)
            odd.append(jnp.where(paired, value, 0.0) - other)
        even = jnp.concatenate(even, axis=1)
        odd = jnp.concatenate(odd, axis=1)

        real = [jnp.concatenate([even.astype(jnp.bfloat16), jnp.zeros(even.shape, jnp.bfloat16)], 1)]
        imag = [jnp.concatenate([jnp.zeros(odd.shape, jnp.bfloat16), odd.astype(jnp.bfloat16)], 1)]
        for g in range(1, groups):
            c = twc_ref[pl.ds(j * groups + g, 1), :]
            s = tws_ref[pl.ds(j * groups + g, 1), :]
            real.append(
                jnp.concatenate(
                    [(even * c).astype(jnp.bfloat16), (even * -s).astype(jnp.bfloat16)], axis=1
                )
            )
            imag.append(
                jnp.concatenate(
                    [(odd * s).astype(jnp.bfloat16), (odd * c).astype(jnp.bfloat16)], axis=1
                )
            )
        left = jnp.concatenate(real + imag, axis=0)

        products.append(jnp.dot(left, t_ref[j], preferred_element_type=jnp.float32))
    for j in range(rows):
        product = products[j]
        for g in range(groups):
            yr = product[g * pad:(g + 1) * pad]
            yi = product[(groups + g) * pad:(groups + g + 1) * pad]
            c = turn_ref[0, pl.ds(j, 1), pl.ds(g * LANES, LANES)]
            s = turn_ref[1, pl.ds(j, 1), pl.ds(g * LANES, LANES)]
            e_ref[g, pl.ds(j * 2 * pairs, pairs, stride=2), :] = (c * yr + s * yi)[:pairs]
            e_ref[g, pl.ds(j * 2 * pairs + 1, pairs, stride=2), :] = (s * yr - c * yi)[:pairs]

    select = (
        iota((wave_total, wave_total), 0) == order_ref[...]
    ).astype(jnp.float32).astype(jnp.bfloat16)
    fourier = jnp.concatenate([e_ref[g].astype(jnp.bfloat16) for g in range(groups)], axis=1)
    slots = jnp.dot(fourier, select, preferred_element_type=jnp.float32)
    used = rows * 2 * pairs
    spare = LANES - used
    if mix:
        chunks = used // spare
        moved = out_ref.shape[2]
        slot_count = moved * (chunks + 1)
        slot = iota((spare, wave_total), 1) % slot_count
        extra = jnp.zeros((spare, wave_total), jnp.float32)
        for q in range(chunks):
            shift = LANES - (chunks - q) * moved
            part = jnp.concatenate(
                [
                    pltpu.roll(
                        slots[q * spare:(q + 1) * spare, g * LANES:(g + 1) * LANES], shift, 1
                    )
                    for g in range(groups)
                ],
                axis=1,
            )
            extra = jnp.where(slot // moved == q, part, extra)
        payload = jnp.concatenate([slots, extra], axis=0).T
        payload = payload.reshape(wave_total // slot_count, chunks + 1, moved, LANES)
        out_ref[...] = payload[:, :chunks].astype(jnp.bfloat16)
    else:
        blank = jnp.zeros((spare, wave_total), jnp.float32)
        out_ref[...] = jnp.concatenate([slots, blank], axis=0).T.astype(jnp.bfloat16)
    if mix:
        fetch.wait()


def spectral_kernel(
    axes, sources, packed, groups, order_ref, recv_ref, table_ref, out_hbm,
    g_ref, left_ref, out_ref, sems,
):
    peers, fields, levels, slot_count, _, wave_total = out_ref.shape
    row_total = table_ref.shape[-1]
    rows = row_total // sources
    height = 2 * fields * levels
    used = rows * height
    spare = LANES - used
    g_ref[...] = recv_ref[...].astype(jnp.float32).reshape(g_ref.shape)

    spread = (
        iota((sources, row_total), 0) == iota((sources, row_total), 1) // rows
    ).astype(jnp.float32).astype(jnp.bfloat16)
    lane_row = iota((height, row_total), 1) % rows
    sent = g_ref.shape[1] // sources
    for peer in range(peers):
        turned = [
            g_ref[peer, pl.ds(slot, sources, stride=sent), :].T.astype(jnp.bfloat16)
            for slot in range(sent)
        ]
        blocks = [value[:used] for value in turned]
        if packed:
            moved = slot_count - sent
            for t in range(moved):
                blocks.append(
                    jnp.concatenate([value[used:] for value in turned[t::moved]], axis=0)
                )
        expanded = jnp.dot(
            jnp.concatenate(blocks, axis=0), spread, preferred_element_type=jnp.float32
        )
        for slot in range(slot_count):
            at = slot * used
            left = expanded[at:at + height]
            for j in range(1, rows):
                at = slot * used + j * height
                left = jnp.where(lane_row == j, expanded[at:at + height], left)
            left_ref[peer, slot] = left.astype(jnp.bfloat16)

    shard = lax.axis_index(axes[0]) * lax.axis_size(axes[1]) + lax.axis_index(axes[1])
    shape = (slot_count, order_ref.shape[1])
    own = lax.broadcasted_iota(jnp.int32, shape, 1) == (
        lax.broadcasted_iota(jnp.int32, shape, 0) + shard * slot_count
    )
    orders = jnp.where(own, order_ref[...].astype(jnp.float32), 0.0)
    orders = jnp.sum(orders, axis=1, keepdims=True).astype(jnp.int32)

    degrees = iota((height, wave_total), 1)
    copies = []
    done = 0
    for slot in range(slot_count):
        order = orders[slot:slot + 1]
        for peer in range(peers):
            value = lax.dot_general(
                left_ref[peer, slot], table_ref[slot], (((1,), (1,)), ((), ())),
                preferred_element_type=jnp.float32,
            )
            value = jnp.where(degrees >= order, value, 0.0)
            for field in range(fields):
                for level in range(levels):
                    at = 2 * (field * levels + level)
                    out_ref[peer, field, level, slot] = value[at:at + 2]
        if slot + 1 in groups:
            at = (slice(None), slice(None), slice(None), pl.ds(done, slot + 1 - done))
            copies.append(
                pltpu.make_async_copy(out_ref.at[at], out_hbm.at[at], sems.at[len(copies)])
            )
            copies[-1].start()
            done = slot + 1
    for copy in copies:
        copy.wait()


def body(grid_adjoint, courant, row_points, wave_order, legendre, vert_inverse):
    fields, levels_dev, row_count, row_width = grid_adjoint.shape
    wave_total = wave_order.shape[0]
    groups = wave_total // LANES
    sources = lax.axis_size("wave")
    peers = lax.axis_size("lev")
    pad = -(-fields * levels_dev // 16) * 16
    mix = peers == 1
    smem = pl.BlockSpec(memory_space=pltpu.SMEM)
    vmem = pl.BlockSpec(memory_space=pltpu.VMEM)
    slot_count = wave_total // sources
    used = row_count * 2 * fields * levels_dev
    chunks = used // (LANES - used)
    moved = slot_count // (chunks + 1)
    packet = (sources, chunks, moved, LANES) if mix else (wave_total, LANES)
    hbm = pl.BlockSpec(memory_space=pl.ANY)
    out_shape = [pltpu.VMEM(packet, jnp.bfloat16)]
    tiles = row_width // LANES
    half_tiles = -(-row_width // (2 * LANES))
    half_width = half_tiles * LANES
    blocks = half_width // (2 * HALF)
    scratch = [
        pltpu.VMEM(grid_adjoint.shape, grid_adjoint.dtype),
        pltpu.VMEM(courant.shape, courant.dtype),
        pltpu.VMEM((row_count, tiles, pad, LANES), jnp.float32),
        pltpu.VMEM((row_count, tiles + 2, pad, LANES), jnp.float32),
        pltpu.VMEM((row_count, half_tiles + tiles, pad, LANES), jnp.float32),
        pltpu.VMEM((row_count, 2 * half_width, LANES), jnp.bfloat16),
        pltpu.VMEM((groups, used, LANES), jnp.float32),
        pltpu.VMEM((row_count * groups, half_width), jnp.float32),
        pltpu.VMEM((row_count * groups, half_width), jnp.float32),
        pltpu.VMEM((row_count, blocks, LANES), jnp.float32),
        pltpu.VMEM((row_count, blocks, LANES), jnp.float32),
        pltpu.VMEM((2, max(row_count, 8), wave_total), jnp.float32),
        pltpu.VMEM((pad, LANES), jnp.float32),
        pltpu.SMEM(row_points.shape, row_points.dtype),
        pltpu.SMEM(vert_inverse.shape, vert_inverse.dtype),
        pltpu.VMEM((1, wave_total), jnp.int32),
        *[pltpu.SemaphoreType.DMA(())] * 5,
    ]
    operands = [row_points, vert_inverse, grid_adjoint, courant, wave_order.reshape(1, wave_total)]
    specs = [hbm] * 5
    if mix:
        operands.append(legendre)
        specs.append(hbm)
        out_shape.append(pltpu.VMEM(legendre.shape, legendre.dtype))
        scratch.append(pltpu.SemaphoreType.DMA(()))
    send, *table = pl.pallas_call(
        lambda *refs: grid_kernel(mix, pad, *refs),
        out_shape=out_shape,
        in_specs=specs,
        out_specs=[vmem] * len(out_shape),
        scratch_shapes=scratch,
        name="grid_side",
    )(*operands)

    received = lax.all_to_all(send, "wave", split_axis=0, concat_axis=0, tiled=True)
    sent = chunks * moved
    if peers > 1:
        received = received.reshape(1, sources, slot_count, LANES)
        table = [lax.all_to_all(legendre, "lev", split_axis=0, concat_axis=1, tiled=True)]
        received = lax.all_to_all(received, "lev", split_axis=2, concat_axis=0, tiled=True)
    slot_count, degrees, row_total = table[0].shape
    if peers > 1:
        sent = slot_count
        received = received.reshape(peers, sources * sent, LANES)
    block = math.gcd(4, slot_count)
    ends = tuple(range(block, slot_count + 1, block))
    shape = (peers, fields, levels_dev, slot_count, 2, degrees)
    out = pl.pallas_call(
        lambda *refs: spectral_kernel(("wave", "lev"), sources, mix, ends, *refs),
        out_shape=jax.ShapeDtypeStruct(shape, jnp.float32),
        in_specs=[vmem, vmem, vmem],
        out_specs=hbm,
        scratch_shapes=[
            pltpu.VMEM((peers, sources * sent, LANES), jnp.float32),
            pltpu.VMEM((peers, slot_count, 2 * fields * levels_dev, row_total), jnp.bfloat16),
            pltpu.VMEM(shape, jnp.float32),
            pltpu.SemaphoreType.DMA((len(ends),)),
        ],
        compiler_params=pltpu.CompilerParams(vmem_limit_bytes=16 << 20),
        name="spectral_side",
    )(
        wave_order.reshape(1, wave_total),
        pltpu.with_memory_space_constraint(received, pltpu.VMEM),
        pltpu.with_memory_space_constraint(table[0], pltpu.VMEM),
    )
    if mix:
        return out[0]
    out = jnp.transpose(out, (1, 0, 2, 3, 4, 5)).reshape(
        fields, peers * levels_dev, slot_count, 2, degrees
    )
    return jnp.einsum("fpl,fpicn->flicn", vert_inverse, out, precision=lax.Precision.HIGHEST)


def solution(mesh):
    return jax.shard_map(
        body,
        mesh=mesh,
        in_specs=(
            P(None, "lev", "wave", None),
            P("lev", "wave", None),
            P("wave"),
            P(),
            P("wave", "lev", None),
            P(),
        ),
        out_specs=P(None, None, ("wave", "lev"), None, None),
        check_vma=False,
    )
```

```python
import math

import jax
import jax.numpy as jnp
from jax import lax
from jax.experimental import pallas as pl
from jax.experimental.pallas import tpu as pltpu
from jax.sharding import PartitionSpec as P

LANES = 128
HALF = 16
SIN_COEFFS = tuple(
    (-1.0) ** i * (2.0 * math.pi) ** (2 * i + 1) / math.factorial(2 * i + 1) for i in range(6)
)


def sin_quarter(v):
    s = v * v
    acc = SIN_COEFFS[5] * s + SIN_COEFFS[4]
    for c in SIN_COEFFS[3::-1]:
        acc = acc * s + c
    return acc * v


def cos_sin(product, count, inverse):
    turns = jnp.floor(product * inverse + 0.5)
    u = (product - turns * count) * inverse
    cosine = sin_quarter(0.25 - jnp.abs(u))
    sine = sin_quarter(jnp.maximum(jnp.minimum(u, 0.5 - u), -0.5 - u))
    return cosine, sine


def iota(shape, axis):
    return lax.broadcasted_iota(jnp.int32, shape, axis)


def within_tile(lane):
    inner = lane % (2 * HALF)
    return lane - inner + jnp.where(inner < HALF, HALF + inner, 2 * HALF - 1 - inner)


def grid_kernel(
    mix, pad, points_hbm, vert_hbm, grid_hbm, wind_hbm, order_hbm, *rest
):
    if mix:
        table_hbm, out_ref, table_ref, *scratch, table_sem = rest
        fetch = pltpu.make_async_copy(table_hbm, table_ref, table_sem)
    else:
        out_ref, *scratch = rest
    (
        grid_buf, wind_buf, g_ref, f_ref, x_ref, t_ref, e_ref,
        twc_ref, tws_ref, ac_ref, as_ref, turn_ref, mix_ref,
        points_ref, vert_ref, order_ref, points_sem, vert_sem, order_sem, grid_sem, wind_sem,
    ) = scratch
    points_copy = pltpu.make_async_copy(points_hbm, points_ref, points_sem)
    points_copy.start()
    vert_copy = pltpu.make_async_copy(vert_hbm, vert_ref, vert_sem)
    order_copy = pltpu.make_async_copy(order_hbm, order_ref, order_sem)
    grid_copy = pltpu.make_async_copy(grid_hbm, grid_buf, grid_sem)
    wind_copy = pltpu.make_async_copy(wind_hbm, wind_buf, wind_sem)
    grid_copy.start()
    wind_copy.start()
    vert_copy.start()
    order_copy.start()
    if mix:
        fetch.start()
    fields, levels, rows, width = grid_buf.shape
    wave_total = order_ref.shape[1]
    groups = wave_total // LANES
    pairs = fields * levels
    tiles = width // LANES
    half_tiles = -(-width // (2 * LANES))
    half_width = half_tiles * LANES

    points_copy.wait()

    shape = (rows * groups, half_width)
    row_id = iota(shape, 0)
    count = jnp.zeros(shape, jnp.int32)
    for j in range(rows):
        count = jnp.where(row_id // groups == j, 2 * points_ref[j], count)
    count = count.astype(jnp.float32)
    lane = iota(shape, 1)
    product = ((row_id % groups) * LANES * (2 * within_tile(lane) + 1)).astype(jnp.float32)
    twc, tws = cos_sin(product, count, 1.0 / count)
    twc_ref[...] = twc
    tws_ref[...] = tws

    shape = (max(rows, 8), wave_total)
    row_id = iota(shape, 0)
    count = jnp.full(shape, 2 * points_ref[0], jnp.int32)
    for j in range(1, rows):
        count = jnp.where(row_id == j, 2 * points_ref[j], count)
    wave = iota(shape, 1)
    weight = jnp.where(2 * wave > count // 2 - 1, 0.0, jnp.where(wave == 0, 1.0, 2.0))
    count = count.astype(jnp.float32)
    cosine, sine = cos_sin(wave.astype(jnp.float32), count, 1.0 / count)
    turn_ref[0] = cosine * weight
    turn_ref[1] = sine * weight

    blocks = half_width // (2 * HALF)
    high = (iota((blocks, LANES), 1) * (4 * HALF * iota((blocks, LANES), 0) + 2 * HALF)).astype(
        jnp.float32
    )
    low = (iota((HALF, LANES), 1) * (2 * iota((HALF, LANES), 0) + 1)).astype(jnp.float32)
    for j in range(rows):
        count = jnp.full((8, LANES), 2 * points_ref[j], jnp.int32).astype(jnp.float32)
        inverse = (1.0 / count)[:1]
        count = count[:1]
        ac, as_ = cos_sin(high, count, inverse)
        ac_ref[j] = ac
        as_ref[j] = as_
        bc, bs = cos_sin(low, count, inverse)
        for block in range(blocks):
            hc = ac_ref[j, pl.ds(block, 1), :]
            hs = as_ref[j, pl.ds(block, 1), :]
            cc, ss, sc, cs = hc * bc, hs * bs, hs * bc, hc * bs
            at = 2 * HALF * block
            t_ref[j, pl.ds(at, HALF), :] = (cc - ss).astype(jnp.bfloat16)
            t_ref[j, pl.ds(at + HALF, HALF), :] = (cc + ss).astype(jnp.bfloat16)
            at += half_width
            t_ref[j, pl.ds(at, HALF), :] = (sc + cs).astype(jnp.bfloat16)
            t_ref[j, pl.ds(at + HALF, HALF), :] = (sc - cs).astype(jnp.bfloat16)

    vert_copy.wait()
    if mix:
        mix_ref[...] = jnp.zeros_like(mix_ref)
        lane = iota((1, LANES), 1)
        for field in range(fields):
            for level in range(levels):
                row = jnp.zeros((1, LANES), jnp.float32)
                for p in range(levels):
                    hit = (lane % pad == field * levels + p) & (lane < 3 * pad)
                    row = jnp.where(hit, vert_ref[field, p, level], row)
                mix_ref[pl.ds(field * levels + level, 1), :] = row
        full = mix_ref[...]
        first = full.astype(jnp.bfloat16).astype(jnp.float32)
        second = (full - first).astype(jnp.bfloat16).astype(jnp.float32)
        third = full - first - second
        lane = iota((pad, LANES), 1)
        matrix = jnp.where(lane < pad, first, jnp.where(lane < 2 * pad, second, third))
        matrix = matrix[:, :3 * pad].astype(jnp.bfloat16)

    order_copy.wait()
    wind_copy.wait()
    grid_copy.wait()
    half_pad = pad // 2
    shape = (rows * pad, pairs * rows)
    pick = (iota(shape, 0) % pad * rows + iota(shape, 0) // pad == iota(shape, 1)) & (
        iota(shape, 0) % pad < pairs
    )
    grid_rows = jnp.dot(
        pick.astype(jnp.float32).astype(jnp.bfloat16),
        grid_buf[...].reshape(pairs * rows, width),
        preferred_element_type=jnp.float32,
    )
    shape = (rows * half_pad, levels * rows)
    pick = iota(shape, 0) % levels * rows + iota(shape, 0) // half_pad == iota(shape, 1)
    wind_rows = jnp.dot(
        jnp.where(pick, 0.5, 0.0).astype(jnp.bfloat16),
        wind_buf[...].reshape(levels * rows, width),
        preferred_element_type=jnp.float32,
    )
    for j in range(rows):
        for t in range(tiles):
            at = slice(t * LANES, (t + 1) * LANES)
            g = grid_rows[j * pad:(j + 1) * pad, at]
            w = wind_rows[j * half_pad:(j + 1) * half_pad, at]
            g_ref[j, t] = g
            f_ref[j, t] = g * jnp.concatenate([w, w], axis=0)

    lane = iota((pad, LANES), 1)
    point = within_tile(lane)
    advected = []
    for j in range(rows):
        length = points_ref[j]
        last_lane = (length - 1) % LANES
        head = pltpu.roll(f_ref[j, 0], last_lane, 1)
        tail = pltpu.roll(f_ref[j, (length - 1) // LANES], (LANES - last_lane) % LANES, 1)
        flux = [f_ref[j, t] for t in range(tiles)]
        ahead = [pltpu.roll(f, LANES - 1, 1) for f in flux]
        behind = [pltpu.roll(f, 1, 1) for f in flux]
        parts = []
        for t in range(tiles):
            forward = jnp.where(lane == LANES - 1, ahead[(t + 1) % tiles], ahead[t])
            forward = jnp.where(lane == length - 1 - t * LANES, head, forward)
            backward = jnp.where(lane == 0, behind[t - 1] if t else tail, behind[t])
            parts.append((g_ref[j, t] + (forward - backward)).astype(jnp.bfloat16))
        advected.append(jnp.concatenate(parts, axis=1))
    for j in range(rows):
        if mix:
            mixed = jnp.dot(
                matrix, jnp.concatenate([advected[j]] * 3, axis=0),
                preferred_element_type=jnp.float32,
            )
        else:
            mixed = advected[j].astype(jnp.float32)
        for t in range(tiles):
            x_ref[j, half_tiles + t] = mixed[:, t * LANES:(t + 1) * LANES]

    products = []
    for j in range(rows):
        length = points_ref[j]
        last_tile = (length - 1) // LANES
        last_lane = (length - 1) % LANES
        mirror = (last_lane - point) & (LANES - 1)
        mirrored = [
            jnp.take_along_axis(x_ref[j, half_tiles + last_tile - t], mirror, axis=1)
            for t in range(half_tiles + 1)
        ]
        even = []
        odd = []
        for t in range(half_tiles):
            value = jnp.take_along_axis(x_ref[j, half_tiles + t], point, axis=1)
            other = jnp.where(point <= last_lane, mirrored[t], mirrored[t + 1])
            paired = 2 * (point + t * LANES) < length - 1
            kept = 2 * (point + t * LANES) <= length - 1
            other = jnp.where(paired, other, 0.0)
            even.append(jnp.where(kept, value, 0.0) + other)
            odd.append(jnp.where(paired, value, 0.0) - other)
        even = jnp.concatenate(even, axis=1)
        odd = jnp.concatenate(odd, axis=1)

        real = [jnp.concatenate([even.astype(jnp.bfloat16), jnp.zeros(even.shape, jnp.bfloat16)], 1)]
        imag = [jnp.concatenate([jnp.zeros(odd.shape, jnp.bfloat16), odd.astype(jnp.bfloat16)], 1)]
        for g in range(1, groups):
            c = twc_ref[pl.ds(j * groups + g, 1), :]
            s = tws_ref[pl.ds(j * groups + g, 1), :]
            real.append(
                jnp.concatenate(
                    [(even * c).astype(jnp.bfloat16), (even * -s).astype(jnp.bfloat16)], axis=1
                )
            )
            imag.append(
                jnp.concatenate(
                    [(odd * s).astype(jnp.bfloat16), (odd * c).astype(jnp.bfloat16)], axis=1
                )
            )
        left = jnp.concatenate(real + imag, axis=0)

        products.append(jnp.dot(left, t_ref[j], preferred_element_type=jnp.float32))
    for j in range(rows):
        product = products[j]
        for g in range(groups):
            yr = product[g * pad:(g + 1) * pad]
            yi = product[(groups + g) * pad:(groups + g + 1) * pad]
            c = turn_ref[0, pl.ds(j, 1), pl.ds(g * LANES, LANES)]
            s = turn_ref[1, pl.ds(j, 1), pl.ds(g * LANES, LANES)]
            e_ref[g, pl.ds(j * 2 * pairs, pairs, stride=2), :] = (c * yr + s * yi)[:pairs]
            e_ref[g, pl.ds(j * 2 * pairs + 1, pairs, stride=2), :] = (s * yr - c * yi)[:pairs]

    select = (
        iota((wave_total, wave_total), 0) == order_ref[...]
    ).astype(jnp.float32).astype(jnp.bfloat16)
    fourier = jnp.concatenate([e_ref[g].astype(jnp.bfloat16) for g in range(groups)], axis=1)
    slots = jnp.dot(fourier, select, preferred_element_type=jnp.float32)
    used = rows * 2 * pairs
    spare = LANES - used
    if mix:
        chunks = used // spare
        moved = out_ref.shape[2]
        slot_count = moved * (chunks + 1)
        slot = iota((spare, wave_total), 1) % slot_count
        extra = jnp.zeros((spare, wave_total), jnp.float32)
        for q in range(chunks):
            shift = LANES - (chunks - q) * moved
            part = jnp.concatenate(
                [
                    pltpu.roll(
                        slots[q * spare:(q + 1) * spare, g * LANES:(g + 1) * LANES], shift, 1
                    )
                    for g in range(groups)
                ],
                axis=1,
            )
            extra = jnp.where(slot // moved == q, part, extra)
        payload = jnp.concatenate([slots, extra], axis=0).T
        payload = payload.reshape(wave_total // slot_count, chunks + 1, moved, LANES)
        out_ref[...] = payload[:, :chunks].astype(jnp.bfloat16)
    else:
        blank = jnp.zeros((spare, wave_total), jnp.float32)
        out_ref[...] = jnp.concatenate([slots, blank], axis=0).T.astype(jnp.bfloat16)
    if mix:
        fetch.wait()


def spectral_kernel(
    axes, sources, packed, groups, order_ref, recv_ref, table_ref, out_hbm,
    g_ref, left_ref, out_ref, sems,
):
    peers, fields, levels, slot_count, _, wave_total = out_ref.shape
    row_total = table_ref.shape[-1]
    rows = row_total // sources
    height = 2 * fields * levels
    used = rows * height
    spare = LANES - used
    g_ref[...] = recv_ref[...].astype(jnp.float32).reshape(g_ref.shape)

    spread = (
        iota((sources, row_total), 0) == iota((sources, row_total), 1) // rows
    ).astype(jnp.float32).astype(jnp.bfloat16)
    lane_row = iota((height, row_total), 1) % rows
    sent = g_ref.shape[1] // sources
    for peer in range(peers):
        turned = [
            g_ref[peer, pl.ds(slot, sources, stride=sent), :].T.astype(jnp.bfloat16)
            for slot in range(sent)
        ]
        blocks = [value[:used] for value in turned]
        if packed:
            moved = slot_count - sent
            for t in range(moved):
                blocks.append(
                    jnp.concatenate([value[used:] for value in turned[t::moved]], axis=0)
                )
        expanded = jnp.dot(
            jnp.concatenate(blocks, axis=0), spread, preferred_element_type=jnp.float32
        )
        for slot in range(slot_count):
            at = slot * used
            left = expanded[at:at + height]
            for j in range(1, rows):
                at = slot * used + j * height
                left = jnp.where(lane_row == j, expanded[at:at + height], left)
            left_ref[peer, slot] = left.astype(jnp.bfloat16)

    shard = lax.axis_index(axes[0]) * lax.axis_size(axes[1]) + lax.axis_index(axes[1])
    shape = (slot_count, order_ref.shape[1])
    own = lax.broadcasted_iota(jnp.int32, shape, 1) == (
        lax.broadcasted_iota(jnp.int32, shape, 0) + shard * slot_count
    )
    orders = jnp.where(own, order_ref[...].astype(jnp.float32), 0.0)
    orders = jnp.sum(orders, axis=1, keepdims=True).astype(jnp.int32)

    degrees = iota((height, wave_total), 1)
    copies = []
    done = 0
    for slot in range(slot_count):
        order = orders[slot:slot + 1]
        for peer in range(peers):
            value = lax.dot_general(
                left_ref[peer, slot], table_ref[slot], (((1,), (1,)), ((), ())),
                preferred_element_type=jnp.float32,
            )
            value = jnp.where(degrees >= order, value, 0.0)
            for field in range(fields):
                for level in range(levels):
                    at = 2 * (field * levels + level)
                    out_ref[peer, field, level, slot] = value[at:at + 2]
        if slot + 1 in groups:
            at = (slice(None), slice(None), slice(None), pl.ds(done, slot + 1 - done))
            copies.append(
                pltpu.make_async_copy(out_ref.at[at], out_hbm.at[at], sems.at[len(copies)])
            )
            copies[-1].start()
            done = slot + 1
    for copy in copies:
        copy.wait()


def body(grid_adjoint, courant, row_points, wave_order, legendre, vert_inverse):
    fields, levels_dev, row_count, row_width = grid_adjoint.shape
    wave_total = wave_order.shape[0]
    groups = wave_total // LANES
    sources = lax.axis_size("wave")
    peers = lax.axis_size("lev")
    pad = -(-fields * levels_dev // 16) * 16
    mix = peers == 1
    smem = pl.BlockSpec(memory_space=pltpu.SMEM)
    vmem = pl.BlockSpec(memory_space=pltpu.VMEM)
    slot_count = wave_total // sources
    used = row_count * 2 * fields * levels_dev
    chunks = used // (LANES - used)
    moved = slot_count // (chunks + 1)
    packet = (sources, chunks, moved, LANES) if mix else (wave_total, LANES)
    hbm = pl.BlockSpec(memory_space=pl.ANY)
    out_shape = [pltpu.VMEM(packet, jnp.bfloat16)]
    tiles = row_width // LANES
    half_tiles = -(-row_width // (2 * LANES))
    half_width = half_tiles * LANES
    blocks = half_width // (2 * HALF)
    scratch = [
        pltpu.VMEM(grid_adjoint.shape, grid_adjoint.dtype),
        pltpu.VMEM(courant.shape, courant.dtype),
        pltpu.VMEM((row_count, tiles, pad, LANES), jnp.float32),
        pltpu.VMEM((row_count, tiles, pad, LANES), jnp.float32),
        pltpu.VMEM((row_count, half_tiles + tiles, pad, LANES), jnp.float32),
        pltpu.VMEM((row_count, 2 * half_width, LANES), jnp.bfloat16),
        pltpu.VMEM((groups, used, LANES), jnp.float32),
        pltpu.VMEM((row_count * groups, half_width), jnp.float32),
        pltpu.VMEM((row_count * groups, half_width), jnp.float32),
        pltpu.VMEM((row_count, blocks, LANES), jnp.float32),
        pltpu.VMEM((row_count, blocks, LANES), jnp.float32),
        pltpu.VMEM((2, max(row_count, 8), wave_total), jnp.float32),
        pltpu.VMEM((pad, LANES), jnp.float32),
        pltpu.SMEM(row_points.shape, row_points.dtype),
        pltpu.SMEM(vert_inverse.shape, vert_inverse.dtype),
        pltpu.VMEM((1, wave_total), jnp.int32),
        *[pltpu.SemaphoreType.DMA(())] * 5,
    ]
    operands = [row_points, vert_inverse, grid_adjoint, courant, wave_order.reshape(1, wave_total)]
    specs = [hbm] * 5
    if mix:
        operands.append(legendre)
        specs.append(hbm)
        out_shape.append(pltpu.VMEM(legendre.shape, legendre.dtype))
        scratch.append(pltpu.SemaphoreType.DMA(()))
    send, *table = pl.pallas_call(
        lambda *refs: grid_kernel(mix, pad, *refs),
        out_shape=out_shape,
        in_specs=specs,
        out_specs=[vmem] * len(out_shape),
        scratch_shapes=scratch,
        name="grid_side",
    )(*operands)

    received = lax.all_to_all(send, "wave", split_axis=0, concat_axis=0, tiled=True)
    sent = chunks * moved
    if peers > 1:
        received = received.reshape(1, sources, slot_count, LANES)
        table = [lax.all_to_all(legendre, "lev", split_axis=0, concat_axis=1, tiled=True)]
        received = lax.all_to_all(received, "lev", split_axis=2, concat_axis=0, tiled=True)
    slot_count, degrees, row_total = table[0].shape
    if peers > 1:
        sent = slot_count
        received = received.reshape(peers, sources * sent, LANES)
    block = math.gcd(4, slot_count)
    ends = tuple(range(block, slot_count + 1, block))
    shape = (peers, fields, levels_dev, slot_count, 2, degrees)
    out = pl.pallas_call(
        lambda *refs: spectral_kernel(("wave", "lev"), sources, mix, ends, *refs),
        out_shape=jax.ShapeDtypeStruct(shape, jnp.float32),
        in_specs=[vmem, vmem, vmem],
        out_specs=hbm,
        scratch_shapes=[
            pltpu.VMEM((peers, sources * sent, LANES), jnp.float32),
            pltpu.VMEM((peers, slot_count, 2 * fields * levels_dev, row_total), jnp.bfloat16),
            pltpu.VMEM(shape, jnp.float32),
            pltpu.SemaphoreType.DMA((len(ends),)),
        ],
        compiler_params=pltpu.CompilerParams(vmem_limit_bytes=16 << 20),
        name="spectral_side",
    )(
        wave_order.reshape(1, wave_total),
        pltpu.with_memory_space_constraint(received, pltpu.VMEM),
        pltpu.with_memory_space_constraint(table[0], pltpu.VMEM),
    )
    if mix:
        return out[0]
    out = jnp.transpose(out, (1, 0, 2, 3, 4, 5)).reshape(
        fields, peers * levels_dev, slot_count, 2, degrees
    )
    return jnp.einsum("fpl,fpicn->flicn", vert_inverse, out, precision=lax.Precision.HIGHEST)


def solution(mesh):
    return jax.shard_map(
        body,
        mesh=mesh,
        in_specs=(
            P(None, "lev", "wave", None),
            P("lev", "wave", None),
            P("wave"),
            P(),
            P("wave", "lev", None),
            P(),
        ),
        out_specs=P(None, None, ("wave", "lev"), None, None),
        check_vma=False,
    )
```

```python
import math

import jax
import jax.numpy as jnp
from jax import lax
from jax.experimental import pallas as pl
from jax.experimental.pallas import tpu as pltpu
from jax.sharding import PartitionSpec as P

LANES = 128
HALF = 16
SIN_COEFFS = tuple(
    (-1.0) ** i * (2.0 * math.pi) ** (2 * i + 1) / math.factorial(2 * i + 1) for i in range(6)
)


def sin_quarter(v):
    s = v * v
    acc = SIN_COEFFS[5] * s + SIN_COEFFS[4]
    for c in SIN_COEFFS[3::-1]:
        acc = acc * s + c
    return acc * v


def cos_sin(product, count, inverse):
    turns = jnp.floor(product * inverse + 0.5)
    u = (product - turns * count) * inverse
    cosine = sin_quarter(0.25 - jnp.abs(u))
    sine = sin_quarter(jnp.maximum(jnp.minimum(u, 0.5 - u), -0.5 - u))
    return cosine, sine


def iota(shape, axis):
    return lax.broadcasted_iota(jnp.int32, shape, axis)


def within_tile(lane):
    inner = lane % (2 * HALF)
    return lane - inner + jnp.where(inner < HALF, HALF + inner, 2 * HALF - 1 - inner)


def grid_kernel(
    mix, pad, points_hbm, vert_hbm, grid_hbm, wind_hbm, order_hbm, *rest
):
    if mix:
        table_hbm, out_ref, table_ref, *scratch, table_sem = rest
        fetch = pltpu.make_async_copy(table_hbm, table_ref, table_sem)
    else:
        out_ref, *scratch = rest
    (
        grid_buf, wind_buf, g_ref, f_ref, x_ref, t_ref, e_ref,
        twc_ref, tws_ref, ac_ref, as_ref, turn_ref, mix_ref,
        points_ref, vert_ref, order_ref, points_sem, vert_sem, order_sem, grid_sem, wind_sem,
    ) = scratch
    points_copy = pltpu.make_async_copy(points_hbm, points_ref, points_sem)
    points_copy.start()
    vert_copy = pltpu.make_async_copy(vert_hbm, vert_ref, vert_sem)
    order_copy = pltpu.make_async_copy(order_hbm, order_ref, order_sem)
    grid_copy = pltpu.make_async_copy(grid_hbm, grid_buf, grid_sem)
    wind_copy = pltpu.make_async_copy(wind_hbm, wind_buf, wind_sem)
    grid_copy.start()
    wind_copy.start()
    vert_copy.start()
    order_copy.start()
    if mix:
        fetch.start()
    fields, levels, rows, width = grid_buf.shape
    wave_total = order_ref.shape[1]
    groups = wave_total // LANES
    pairs = fields * levels
    tiles = width // LANES
    half_tiles = -(-width // (2 * LANES))
    half_width = half_tiles * LANES

    points_copy.wait()

    shape = (rows * groups, half_width)
    row_id = iota(shape, 0)
    count = jnp.zeros(shape, jnp.int32)
    for j in range(rows):
        count = jnp.where(row_id // groups == j, 2 * points_ref[j], count)
    count = count.astype(jnp.float32)
    lane = iota(shape, 1)
    product = ((row_id % groups) * LANES * (2 * within_tile(lane) + 1)).astype(jnp.float32)
    twc, tws = cos_sin(product, count, 1.0 / count)
    twc_ref[...] = twc
    tws_ref[...] = tws

    shape = (max(rows, 8), wave_total)
    row_id = iota(shape, 0)
    count = jnp.full(shape, 2 * points_ref[0], jnp.int32)
    for j in range(1, rows):
        count = jnp.where(row_id == j, 2 * points_ref[j], count)
    wave = iota(shape, 1)
    weight = jnp.where(2 * wave > count // 2 - 1, 0.0, jnp.where(wave == 0, 1.0, 2.0))
    count = count.astype(jnp.float32)
    cosine, sine = cos_sin(wave.astype(jnp.float32), count, 1.0 / count)
    turn_ref[0] = cosine * weight
    turn_ref[1] = sine * weight

    blocks = half_width // (2 * HALF)
    high = (iota((blocks, LANES), 1) * (4 * HALF * iota((blocks, LANES), 0) + 2 * HALF)).astype(
        jnp.float32
    )
    low = (iota((HALF, LANES), 1) * (2 * iota((HALF, LANES), 0) + 1)).astype(jnp.float32)
    for j in range(rows):
        count = jnp.full((8, LANES), 2 * points_ref[j], jnp.int32).astype(jnp.float32)
        inverse = (1.0 / count)[:1]
        count = count[:1]
        ac, as_ = cos_sin(high, count, inverse)
        ac_ref[j] = ac
        as_ref[j] = as_
        bc, bs = cos_sin(low, count, inverse)
        for block in range(blocks):
            hc = ac_ref[j, pl.ds(block, 1), :]
            hs = as_ref[j, pl.ds(block, 1), :]
            cc, ss, sc, cs = hc * bc, hs * bs, hs * bc, hc * bs
            at = 2 * HALF * block
            t_ref[j, pl.ds(at, HALF), :] = (cc - ss).astype(jnp.bfloat16)
            t_ref[j, pl.ds(at + HALF, HALF), :] = (cc + ss).astype(jnp.bfloat16)
            at += half_width
            t_ref[j, pl.ds(at, HALF), :] = (sc + cs).astype(jnp.bfloat16)
            t_ref[j, pl.ds(at + HALF, HALF), :] = (sc - cs).astype(jnp.bfloat16)

    vert_copy.wait()
    if mix:
        mix_ref[...] = jnp.zeros_like(mix_ref)
        lane = iota((1, LANES), 1)
        for field in range(fields):
            for level in range(levels):
                row = jnp.zeros((1, LANES), jnp.float32)
                for p in range(levels):
                    hit = (lane % pad == field * levels + p) & (lane < 3 * pad)
                    row = jnp.where(hit, vert_ref[field, p, level], row)
                mix_ref[pl.ds(field * levels + level, 1), :] = row
        full = mix_ref[...]
        first = full.astype(jnp.bfloat16).astype(jnp.float32)
        second = (full - first).astype(jnp.bfloat16).astype(jnp.float32)
        third = full - first - second
        lane = iota((pad, LANES), 1)
        matrix = jnp.where(lane < pad, first, jnp.where(lane < 2 * pad, second, third))
        matrix = matrix[:, :3 * pad].astype(jnp.bfloat16)

    order_copy.wait()
    wind_copy.wait()
    grid_copy.wait()
    half_pad = pad // 2
    shape = (rows * pad, pairs * rows)
    pick = (iota(shape, 0) % pad * rows + iota(shape, 0) // pad == iota(shape, 1)) & (
        iota(shape, 0) % pad < pairs
    )
    grid_rows = jnp.dot(
        pick.astype(jnp.float32).astype(jnp.bfloat16),
        grid_buf[...].reshape(pairs * rows, width),
        preferred_element_type=jnp.float32,
    )
    shape = (rows * half_pad, levels * rows)
    pick = iota(shape, 0) % levels * rows + iota(shape, 0) // half_pad == iota(shape, 1)
    wind_rows = jnp.dot(
        jnp.where(pick, 0.5, 0.0).astype(jnp.bfloat16),
        wind_buf[...].reshape(levels * rows, width),
        preferred_element_type=jnp.float32,
    )
    for j in range(rows):
        for t in range(tiles):
            at = slice(t * LANES, (t + 1) * LANES)
            g = grid_rows[j * pad:(j + 1) * pad, at]
            w = wind_rows[j * half_pad:(j + 1) * half_pad, at]
            g_ref[j, t] = g
            f_ref[j, t] = g * jnp.concatenate([w, w], axis=0)

    lane = iota((pad, LANES), 1)
    point = within_tile(lane)
    advected = []
    for j in range(rows):
        length = points_ref[j]
        last_lane = (length - 1) % LANES
        head = pltpu.roll(f_ref[j, 0], last_lane, 1)
        tail = pltpu.roll(f_ref[j, (length - 1) // LANES], (LANES - last_lane) % LANES, 1)
        flux = [f_ref[j, t] for t in range(tiles)]
        ahead = [pltpu.roll(f, LANES - 1, 1) for f in flux]
        behind = [pltpu.roll(f, 1, 1) for f in flux]
        parts = []
        for t in range(tiles):
            forward = jnp.where(lane == LANES - 1, ahead[(t + 1) % tiles], ahead[t])
            forward = jnp.where(lane == length - 1 - t * LANES, head, forward)
            backward = jnp.where(lane == 0, behind[t - 1] if t else tail, behind[t])
            parts.append((g_ref[j, t] + (forward - backward)).astype(jnp.bfloat16))
        advected.append(jnp.concatenate(parts, axis=1))
        if mix:
            mixed = jnp.dot(
                matrix, jnp.concatenate([advected[j]] * 3, axis=0),
                preferred_element_type=jnp.float32,
            )
        else:
            mixed = advected[j].astype(jnp.float32)
        for t in range(tiles):
            x_ref[j, half_tiles + t] = mixed[:, t * LANES:(t + 1) * LANES]

    products = []
    for j in range(rows):
        length = points_ref[j]
        last_tile = (length - 1) // LANES
        last_lane = (length - 1) % LANES
        mirror = (last_lane - point) & (LANES - 1)
        mirrored = [
            jnp.take_along_axis(x_ref[j, half_tiles + last_tile - t], mirror, axis=1)
            for t in range(half_tiles + 1)
        ]
        even = []
        odd = []
        for t in range(half_tiles):
            value = jnp.take_along_axis(x_ref[j, half_tiles + t], point, axis=1)
            other = jnp.where(point <= last_lane, mirrored[t], mirrored[t + 1])
            paired = 2 * (point + t * LANES) < length - 1
            kept = 2 * (point + t * LANES) <= length - 1
            other = jnp.where(paired, other, 0.0)
            even.append(jnp.where(kept, value, 0.0) + other)
            odd.append(jnp.where(paired, value, 0.0) - other)
        even = jnp.concatenate(even, axis=1)
        odd = jnp.concatenate(odd, axis=1)

        real = [jnp.concatenate([even.astype(jnp.bfloat16), jnp.zeros(even.shape, jnp.bfloat16)], 1)]
        imag = [jnp.concatenate([jnp.zeros(odd.shape, jnp.bfloat16), odd.astype(jnp.bfloat16)], 1)]
        for g in range(1, groups):
            c = twc_ref[pl.ds(j * groups + g, 1), :]
            s = tws_ref[pl.ds(j * groups + g, 1), :]
            real.append(
                jnp.concatenate(
                    [(even * c).astype(jnp.bfloat16), (even * -s).astype(jnp.bfloat16)], axis=1
                )
            )
            imag.append(
                jnp.concatenate(
                    [(odd * s).astype(jnp.bfloat16), (odd * c).astype(jnp.bfloat16)], axis=1
                )
            )
        left = jnp.concatenate(real + imag, axis=0)

        products.append(jnp.dot(left, t_ref[j], preferred_element_type=jnp.float32))
    for j in range(rows):
        product = products[j]
        for g in range(groups):
            yr = product[g * pad:(g + 1) * pad]
            yi = product[(groups + g) * pad:(groups + g + 1) * pad]
            c = turn_ref[0, pl.ds(j, 1), pl.ds(g * LANES, LANES)]
            s = turn_ref[1, pl.ds(j, 1), pl.ds(g * LANES, LANES)]
            e_ref[g, pl.ds(j * 2 * pairs, pairs, stride=2), :] = (c * yr + s * yi)[:pairs]
            e_ref[g, pl.ds(j * 2 * pairs + 1, pairs, stride=2), :] = (s * yr - c * yi)[:pairs]

    select = (
        iota((wave_total, wave_total), 0) == order_ref[...]
    ).astype(jnp.float32).astype(jnp.bfloat16)
    fourier = jnp.concatenate([e_ref[g].astype(jnp.bfloat16) for g in range(groups)], axis=1)
    slots = jnp.dot(fourier, select, preferred_element_type=jnp.float32)
    used = rows * 2 * pairs
    spare = LANES - used
    if mix:
        chunks = used // spare
        moved = out_ref.shape[2]
        slot_count = moved * (chunks + 1)
        slot = iota((spare, wave_total), 1) % slot_count
        extra = jnp.zeros((spare, wave_total), jnp.float32)
        for q in range(chunks):
            shift = LANES - (chunks - q) * moved
            part = jnp.concatenate(
                [
                    pltpu.roll(
                        slots[q * spare:(q + 1) * spare, g * LANES:(g + 1) * LANES], shift, 1
                    )
                    for g in range(groups)
                ],
                axis=1,
            )
            extra = jnp.where(slot // moved == q, part, extra)
        payload = jnp.concatenate([slots, extra], axis=0).T
        payload = payload.reshape(wave_total // slot_count, chunks + 1, moved, LANES)
        out_ref[...] = payload[:, :chunks].astype(jnp.bfloat16)
    else:
        blank = jnp.zeros((spare, wave_total), jnp.float32)
        out_ref[...] = jnp.concatenate([slots, blank], axis=0).T.astype(jnp.bfloat16)
    if mix:
        fetch.wait()


def spectral_kernel(
    axes, sources, packed, groups, order_ref, recv_ref, table_ref, out_hbm,
    g_ref, left_ref, out_ref, sems,
):
    peers, fields, levels, slot_count, _, wave_total = out_ref.shape
    row_total = table_ref.shape[-1]
    rows = row_total // sources
    height = 2 * fields * levels
    used = rows * height
    spare = LANES - used
    g_ref[...] = recv_ref[...].astype(jnp.float32).reshape(g_ref.shape)

    spread = (
        iota((sources, row_total), 0) == iota((sources, row_total), 1) // rows
    ).astype(jnp.float32).astype(jnp.bfloat16)
    lane_row = iota((height, row_total), 1) % rows
    sent = g_ref.shape[1] // sources
    for peer in range(peers):
        turned = [
            g_ref[peer, pl.ds(slot, sources, stride=sent), :].T.astype(jnp.bfloat16)
            for slot in range(sent)
        ]
        blocks = [value[:used] for value in turned]
        if packed:
            moved = slot_count - sent
            for t in range(moved):
                blocks.append(
                    jnp.concatenate([value[used:] for value in turned[t::moved]], axis=0)
                )
        expanded = jnp.dot(
            jnp.concatenate(blocks, axis=0), spread, preferred_element_type=jnp.float32
        )
        for slot in range(slot_count):
            at = slot * used
            left = expanded[at:at + height]
            for j in range(1, rows):
                at = slot * used + j * height
                left = jnp.where(lane_row == j, expanded[at:at + height], left)
            left_ref[peer, slot] = left.astype(jnp.bfloat16)

    shard = lax.axis_index(axes[0]) * lax.axis_size(axes[1]) + lax.axis_index(axes[1])
    shape = (slot_count, order_ref.shape[1])
    own = lax.broadcasted_iota(jnp.int32, shape, 1) == (
        lax.broadcasted_iota(jnp.int32, shape, 0) + shard * slot_count
    )
    orders = jnp.where(own, order_ref[...].astype(jnp.float32), 0.0)
    orders = jnp.sum(orders, axis=1, keepdims=True).astype(jnp.int32)

    degrees = iota((height, wave_total), 1)
    copies = []
    done = 0
    for slot in range(slot_count):
        order = orders[slot:slot + 1]
        for peer in range(peers):
            value = lax.dot_general(
                left_ref[peer, slot], table_ref[slot], (((1,), (1,)), ((), ())),
                preferred_element_type=jnp.float32,
            )
            value = jnp.where(degrees >= order, value, 0.0)
            for field in range(fields):
                for level in range(levels):
                    at = 2 * (field * levels + level)
                    out_ref[peer, field, level, slot] = value[at:at + 2]
        if slot + 1 in groups:
            at = (slice(None), slice(None), slice(None), pl.ds(done, slot + 1 - done))
            copies.append(
                pltpu.make_async_copy(out_ref.at[at], out_hbm.at[at], sems.at[len(copies)])
            )
            copies[-1].start()
            done = slot + 1
    for copy in copies:
        copy.wait()


def body(grid_adjoint, courant, row_points, wave_order, legendre, vert_inverse):
    fields, levels_dev, row_count, row_width = grid_adjoint.shape
    wave_total = wave_order.shape[0]
    groups = wave_total // LANES
    sources = lax.axis_size("wave")
    peers = lax.axis_size("lev")
    pad = -(-fields * levels_dev // 16) * 16
    mix = peers == 1
    smem = pl.BlockSpec(memory_space=pltpu.SMEM)
    vmem = pl.BlockSpec(memory_space=pltpu.VMEM)
    slot_count = wave_total // sources
    used = row_count * 2 * fields * levels_dev
    chunks = used // (LANES - used)
    moved = slot_count // (chunks + 1)
    packet = (sources, chunks, moved, LANES) if mix else (wave_total, LANES)
    hbm = pl.BlockSpec(memory_space=pl.ANY)
    out_shape = [pltpu.VMEM(packet, jnp.bfloat16)]
    tiles = row_width // LANES
    half_tiles = -(-row_width // (2 * LANES))
    half_width = half_tiles * LANES
    blocks = half_width // (2 * HALF)
    scratch = [
        pltpu.VMEM(grid_adjoint.shape, grid_adjoint.dtype),
        pltpu.VMEM(courant.shape, courant.dtype),
        pltpu.VMEM((row_count, tiles, pad, LANES), jnp.float32),
        pltpu.VMEM((row_count, tiles, pad, LANES), jnp.float32),
        pltpu.VMEM((row_count, half_tiles + tiles, pad, LANES), jnp.float32),
        pltpu.VMEM((row_count, 2 * half_width, LANES), jnp.bfloat16),
        pltpu.VMEM((groups, used, LANES), jnp.float32),
        pltpu.VMEM((row_count * groups, half_width), jnp.float32),
        pltpu.VMEM((row_count * groups, half_width), jnp.float32),
        pltpu.VMEM((row_count, blocks, LANES), jnp.float32),
        pltpu.VMEM((row_count, blocks, LANES), jnp.float32),
        pltpu.VMEM((2, max(row_count, 8), wave_total), jnp.float32),
        pltpu.VMEM((pad, LANES), jnp.float32),
        pltpu.SMEM(row_points.shape, row_points.dtype),
        pltpu.SMEM(vert_inverse.shape, vert_inverse.dtype),
        pltpu.VMEM((1, wave_total), jnp.int32),
        *[pltpu.SemaphoreType.DMA(())] * 5,
    ]
    operands = [row_points, vert_inverse, grid_adjoint, courant, wave_order.reshape(1, wave_total)]
    specs = [hbm] * 5
    if mix:
        operands.append(legendre)
        specs.append(hbm)
        out_shape.append(pltpu.VMEM(legendre.shape, legendre.dtype))
        scratch.append(pltpu.SemaphoreType.DMA(()))
    send, *table = pl.pallas_call(
        lambda *refs: grid_kernel(mix, pad, *refs),
        out_shape=out_shape,
        in_specs=specs,
        out_specs=[vmem] * len(out_shape),
        scratch_shapes=scratch,
        name="grid_side",
    )(*operands)

    received = lax.all_to_all(send, "wave", split_axis=0, concat_axis=0, tiled=True)
    sent = chunks * moved
    if peers > 1:
        received = received.reshape(1, sources, slot_count, LANES)
        table = [lax.all_to_all(legendre, "lev", split_axis=0, concat_axis=1, tiled=True)]
        received = lax.all_to_all(received, "lev", split_axis=2, concat_axis=0, tiled=True)
    slot_count, degrees, row_total = table[0].shape
    if peers > 1:
        sent = slot_count
        received = received.reshape(peers, sources * sent, LANES)
    block = math.gcd(4, slot_count)
    ends = tuple(range(block, slot_count + 1, block))
    shape = (peers, fields, levels_dev, slot_count, 2, degrees)
    out = pl.pallas_call(
        lambda *refs: spectral_kernel(("wave", "lev"), sources, mix, ends, *refs),
        out_shape=jax.ShapeDtypeStruct(shape, jnp.float32),
        in_specs=[vmem, vmem, vmem],
        out_specs=hbm,
        scratch_shapes=[
            pltpu.VMEM((peers, sources * sent, LANES), jnp.float32),
            pltpu.VMEM((peers, slot_count, 2 * fields * levels_dev, row_total), jnp.bfloat16),
            pltpu.VMEM(shape, jnp.float32),
            pltpu.SemaphoreType.DMA((len(ends),)),
        ],
        compiler_params=pltpu.CompilerParams(vmem_limit_bytes=16 << 20),
        name="spectral_side",
    )(
        wave_order.reshape(1, wave_total),
        pltpu.with_memory_space_constraint(received, pltpu.VMEM),
        pltpu.with_memory_space_constraint(table[0], pltpu.VMEM),
    )
    if mix:
        return out[0]
    out = jnp.transpose(out, (1, 0, 2, 3, 4, 5)).reshape(
        fields, peers * levels_dev, slot_count, 2, degrees
    )
    return jnp.einsum("fpl,fpicn->flicn", vert_inverse, out, precision=lax.Precision.HIGHEST)


def solution(mesh):
    return jax.shard_map(
        body,
        mesh=mesh,
        in_specs=(
            P(None, "lev", "wave", None),
            P("lev", "wave", None),
            P("wave"),
            P(),
            P("wave", "lev", None),
            P(),
        ),
        out_specs=P(None, None, ("wave", "lev"), None, None),
        check_vma=False,
    )
```
